128 devices in a mesh: row: 32 (over z, x, core), grp: 4 (over y).
Axes of the slice: x: 4, y: 4, z: 4, core: 2. Of those that a mesh axis runs over, the one named last changes fastest.
Arguments:
- features: bfloat16 [262144, 768], P(('row', 'grp')), may hold values from -6 to 6
- dense_edge_weights: bfloat16 [1024, 4, 256, 256], P(('row', 'grp')), may hold values from -0.125 to 0.125
- dense_cols: int32 [1024, 4], P(('row', 'grp')), may hold values from 0 to 7
- dense_ids: int32 [8], replicated, may hold values from 0 to 1023, as said below
- sparse_w: bfloat16 [262144, 1024], P(('row', 'grp')), may hold values from -0.125 to 0.125
- sparse_rows: int32 [128, 128, 8], P(('row', 'grp')), may hold values from 0 to 2047, as said below
- sparse_counts: int32 [128, 128], P(('row', 'grp')), may hold values from 1 to 8, as said below
- weight: bfloat16 [768, 768], replicated, may hold values from -0.21875 to 0.21875
- bias: float32 [768], replicated, may hold values from -3 to 3
Outputs:
- output: bfloat16 [262144, 768], P(('row', 'grp'))
The draws below stay inside these ranges and needn't reach their ends.
Inputs may be any that keep to these rules, and one draw needn't show every extreme that they name: `dense_ids`: distinct row block ids; the first and the last row block are both among them. `sparse_rows`: local row indices of the sender. `sparse_counts`: at most 8 rows from one sender to one receiver; one receiver gets 8 rows from every sender.
All inputs are finite; a program needn't handle non-finite values.
Results may differ from the reference program's by a relative error of at most 0.0044.
Values may be sent and summed in bfloat16 or wider, within the bound.
A program may use at most 128 MiB of HBM per device.

```python
import jax
import jax.numpy as jnp
from jax import lax

D = 768
TILE = 256
TPR = 4
NDENSE = 8
SLOT = 8
PEERS = 128
ROWS_DEV = 2048
NODES = 262144
NBLOCKS = 1024


def draw_dense_ids(key, part):
    first_key = jax.random.fold_in(key, 11)
    second_key = jax.random.fold_in(key, 12)
    middle = 1 + jax.random.permutation(first_key, NBLOCKS - 2)[:NDENSE - 2]
    chosen = jnp.concatenate([jnp.array([NBLOCKS - 1, 0], dtype=jnp.int32), middle.astype(jnp.int32)])
    return chosen[jax.random.permutation(second_key, NDENSE)].astype(jnp.int32)


def draw_sparse_rows(key, part):
    rows_key = jax.random.fold_in(key, 21)
    picked = jax.random.randint(rows_key, (PEERS, PEERS, SLOT), 0, ROWS_DEV, dtype=jnp.int32)
    flat_ids = jnp.arange(PEERS * PEERS * SLOT, dtype=jnp.int32).reshape(PEERS, PEERS, SLOT)
    picked = jnp.where(flat_ids == 0, 0, picked)
    picked = jnp.where(flat_ids == SLOT, ROWS_DEV - 1, picked)
    return picked.astype(jnp.int32)


def draw_sparse_counts(key, part):
    count_key = jax.random.fold_in(key, 31)
    complete_random_key = jax.random.fold_in(key, 32)
    counts = jax.random.randint(count_key, (PEERS, PEERS), 1, SLOT + 1, dtype=jnp.int32)
    complete_target = jax.random.randint(complete_random_key, (), 0, PEERS, dtype=jnp.int32)
    column_ids = jnp.arange(PEERS, dtype=jnp.int32)[None, :]
    return jnp.where(column_ids == complete_target, SLOT, counts).astype(jnp.int32)


def set_ends(values, stream_key, smallest, high):
    dims = values.shape
    index_at = [jax.random.randint(jax.random.fold_in(stream_key, axis), (), 0, dims[axis]) for axis in range(len(dims))]
    values = values.at[tuple(index_at)].set(smallest)
    longest = dims.index(max(dims))
    index_at[longest] = (index_at[longest] + 1) % dims[longest]
    return values.at[tuple(index_at)].set(high)


def block_scale(key, extent, split, smallest, high):
    def one(axis_at, blocks):
        steps = jax.random.uniform(jax.random.fold_in(jax.random.fold_in(key, 6), axis_at), (blocks,), jnp.float32, smallest / len(split), high / len(split))
        return jnp.repeat(jnp.exp(steps), extent[axis_at] // blocks).reshape((-1,) + (1,) * (len(extent) - axis_at - 1))

    gain = one(*split[0])
    for cut in split[1:]:
        gain = gain * one(*cut)
    return gain


def gaussian(own_key, dims, scale, most, pieces=(), held_as=jnp.bfloat16):
    values = jax.random.normal(own_key, dims, jnp.float32) * scale
    if len(pieces) > 0:
        values = block_scale(own_key, dims, pieces, -0.22, 0.18) * values
    return jnp.clip(values, min=-most, max=most).astype(held_as)


def setup_inputs(seed: int = 0) -> dict:
    key_of = jax.random.split(jax.random.key(seed), 10)
    return {
        "features": gaussian(key_of[0], (NODES, D), 1.0, 6.0, ((0, 128),)),
        "dense_edge_weights": gaussian(key_of[1], (NBLOCKS, TPR, TILE, TILE), (TPR * TILE + PEERS * SLOT) ** -0.5, 0.125, ((0, 128),)),
        "dense_cols": set_ends(jax.random.randint(key_of[2], (NBLOCKS, TPR), 0, NDENSE), jax.random.fold_in(key_of[2], 1), 0, NDENSE - 1).astype(jnp.int32),
        "dense_ids": draw_dense_ids(jax.random.fold_in(key_of[9], 71), 0),
        "sparse_w": gaussian(key_of[4], (NODES, PEERS * SLOT), (TPR * TILE + PEERS * SLOT) ** -0.5, 0.125, ((0, 128),)),
        "sparse_rows": draw_sparse_rows(jax.random.fold_in(key_of[9], 71), 0),
        "sparse_counts": draw_sparse_counts(jax.random.fold_in(key_of[9], 71), 0),
        "weight": gaussian(key_of[7], (D, D), D ** -0.5, 0.21875),
        "bias": gaussian(key_of[8], (D,), 0.5, 3.0, (), jnp.float32),
    }


def reference(features, dense_edge_weights, dense_cols, dense_ids, sparse_w, sparse_rows, sparse_counts, weight, bias):
    blocks = features.reshape(NODES // TILE, TILE, D)
    dense_bands = blocks[dense_ids]

    def dense_block(args):
        vals, cols = args
        dense_sum = jnp.zeros((TILE, D), jnp.float32)
        for tile_index in range(TPR):
            dense_sum = dense_sum + jnp.dot(vals[tile_index], dense_bands[cols[tile_index]], preferred_element_type=jnp.float32)
        return dense_sum

    dense_part = lax.map(dense_block, (dense_edge_weights, dense_cols)).reshape(NODES, D)
    owners = features.reshape(PEERS, ROWS_DEV, D)
    slot_ids = jnp.arange(SLOT, dtype=jnp.int32)

    def sparse_dest(args):
        rows_to, counts_to, w_rows = args
        picked = jnp.take_along_axis(owners, rows_to[:, :, None].astype(jnp.int32), axis=1)
        live_slots = slot_ids[None, :] < counts_to[:, None]
        picked = jnp.where(live_slots[:, :, None], picked, jnp.zeros((), picked.dtype))
        return jnp.dot(w_rows, picked.reshape(PEERS * SLOT, D), preferred_element_type=jnp.float32)

    sparse_part = lax.map(sparse_dest, (jnp.transpose(sparse_rows, (1, 0, 2)), jnp.transpose(sparse_counts), sparse_w.reshape(PEERS, ROWS_DEV, PEERS * SLOT)))
    aggregate = (dense_part + sparse_part.reshape(NODES, D)).astype(jnp.bfloat16)
    result = jnp.dot(aggregate, weight, preferred_element_type=jnp.float32) + bias
    return jnp.maximum(result, 0.0).astype(jnp.bfloat16)
```

```python
import jax
import jax.numpy as jnp
from jax import lax
from jax.sharding import PartitionSpec as P

AXES = ("row", "grp")


def on_device(
    features,
    dense_edge_weights,
    dense_cols,
    dense_ids,
    sparse_w,
    sparse_rows,
    sparse_counts,
    weight,
    bias,
):
    block_count = dense_edge_weights.shape[0]
    tiles_per = dense_edge_weights.shape[1]
    tile_size = dense_edge_weights.shape[2]
    feature_width = features.shape[1]
    stripe_count = dense_ids.shape[0]
    local_blocks = features.reshape(block_count, tile_size, feature_width)

    rows_out = sparse_rows[0]
    counts_out = sparse_counts[0]
    peer_count = rows_out.shape[0]
    slot_count = rows_out.shape[1]
    piece = tile_size // peer_count
    me = lax.axis_index(AXES)

    owners = dense_ids // block_count
    mine = owners == me
    candidates = local_blocks[dense_ids % block_count]
    candidates = jnp.where(mine[:, None, None], candidates, jnp.zeros((), candidates.dtype))
    stripe_pieces = candidates.reshape(stripe_count, peer_count, piece, feature_width)
    stripe_pieces = jnp.transpose(stripe_pieces, (1, 0, 2, 3)).reshape(
        peer_count, stripe_count * piece, feature_width
    )

    outgoing = features[rows_out]
    slot_ids = jnp.arange(slot_count, dtype=jnp.int32)
    live_slots = slot_ids[None, :] < counts_out[:, None]
    outgoing = jnp.where(live_slots[:, :, None], outgoing, jnp.zeros((), outgoing.dtype))
    payload = jnp.concatenate([outgoing, stripe_pieces], axis=1)
    arrived = lax.all_to_all(payload, AXES, split_axis=0, concat_axis=0, tiled=True)
    incoming_rows = arrived[:, :slot_count].reshape(peer_count * slot_count, feature_width)
    my_pieces = jnp.sum(arrived[:, slot_count:].astype(jnp.float32), axis=0).astype(jnp.bfloat16)
    gathered = lax.all_gather(my_pieces, AXES, axis=0, tiled=False)
    dense_bands = jnp.transpose(
        gathered.reshape(peer_count, stripe_count, piece, feature_width), (1, 0, 2, 3)
    ).reshape(stripe_count, tile_size, feature_width)

    dense_sum = jnp.zeros((block_count, tile_size, feature_width), jnp.float32)
    for tile_index in range(tiles_per):
        picked_tiles = dense_bands[dense_cols[:, tile_index]]
        dense_sum = dense_sum + jnp.einsum(
            "eim,emh->eih",
            dense_edge_weights[:, tile_index],
            picked_tiles,
            preferred_element_type=jnp.float32,
        )
    sparse_sum = jnp.dot(sparse_w, incoming_rows, preferred_element_type=jnp.float32)
    aggregate = (dense_sum.reshape(block_count * tile_size, feature_width) + sparse_sum).astype(
        jnp.bfloat16
    )
    result = jnp.dot(aggregate, weight, preferred_element_type=jnp.float32) + bias
    return jnp.maximum(result, 0.0).astype(jnp.bfloat16)


def solution(mesh):
    placed = (
        P(AXES, None),
        P(AXES, None, None, None),
        P(AXES, None),
        P(),
        P(AXES, None),
        P(AXES, None, None),
        P(AXES, None),
        P(),
        P(),
    )
    return jax.shard_map(
        on_device, mesh=mesh, in_specs=placed, out_specs=P(AXES, None), check_vma=False
    )
```

```python
import functools

import jax
import jax.numpy as jnp
from jax import lax
from jax.experimental import pallas as pl
from jax.experimental.pallas import tpu as pltpu
from jax.sharding import PartitionSpec as P

AXES = ("row", "grp")


def gather_kernel(group, piece_ref, out_ref, send_sem, recv_sem, local_sem):
    n = out_ref.shape[0]
    me = lax.axis_index(AXES)

    def where(peer):
        return (peer // group, peer % group)

    barrier = pltpu.get_barrier_semaphore()

    def greet(i, carry):
        peer = lax.rem(me + i, n)
        pl.semaphore_signal(barrier, inc=1, device_id=where(peer), device_id_type=pl.DeviceIdType.MESH)
        return carry

    lax.fori_loop(1, n, greet, 0)
    pl.semaphore_wait(barrier, n - 1)
    own = pltpu.make_async_copy(piece_ref, out_ref.at[me], local_sem)
    own.start()

    def send(i, carry):
        peer = lax.rem(me + i, n)
        pltpu.make_async_remote_copy(
            src_ref=piece_ref,
            dst_ref=out_ref.at[me],
            send_sem=send_sem.at[i],
            recv_sem=recv_sem.at[me],
            device_id=where(peer),
            device_id_type=pl.DeviceIdType.MESH,
        ).start()
        return carry

    lax.fori_loop(1, n, send, 0)

    def wait(i, carry):
        peer = lax.rem(me + i, n)
        source = lax.rem(me + n - i, n)
        pltpu.make_async_remote_copy(
            src_ref=piece_ref,
            dst_ref=out_ref.at[source],
            send_sem=send_sem.at[i],
            recv_sem=recv_sem.at[source],
            device_id=where(peer),
            device_id_type=pl.DeviceIdType.MESH,
        ).wait()
        return carry

    lax.fori_loop(1, n, wait, 0)
    own.wait()


def gather_pieces(piece, n, group):
    rows, width = piece.shape
    return pl.pallas_call(
        functools.partial(gather_kernel, group),
        out_shape=jax.ShapeDtypeStruct((n, rows, width), piece.dtype),
        in_specs=[pl.BlockSpec(memory_space=pltpu.VMEM)],
        out_specs=pl.BlockSpec(memory_space=pltpu.VMEM),
        scratch_shapes=[
            pltpu.SemaphoreType.DMA((n,)),
            pltpu.SemaphoreType.DMA((n,)),
            pltpu.SemaphoreType.DMA,
        ],
        compiler_params=pltpu.CompilerParams(collective_id=0, has_side_effects=True),
    )(piece)


def on_device(
    features,
    dense_edge_weights,
    dense_cols,
    dense_ids,
    sparse_w,
    sparse_rows,
    sparse_counts,
    weight,
    bias,
):
    block_count = dense_edge_weights.shape[0]
    tiles_per = dense_edge_weights.shape[1]
    tile_size = dense_edge_weights.shape[2]
    feature_width = features.shape[1]
    stripe_count = dense_ids.shape[0]
    local_blocks = features.reshape(block_count, tile_size, feature_width)
    group = lax.axis_size("grp")

    rows_out = sparse_rows[0]
    counts_out = sparse_counts[0]
    peer_count = rows_out.shape[0]
    slot_count = rows_out.shape[1]
    piece = stripe_count * tile_size // peer_count
    me = lax.axis_index(AXES)

    owners = dense_ids // block_count
    mine = owners == me
    candidates = local_blocks[dense_ids % block_count]
    candidates = jnp.where(mine[:, None, None], candidates, jnp.zeros((), candidates.dtype))
    stripe_pieces = candidates.reshape(peer_count, piece, feature_width)

    outgoing = features[rows_out]
    slot_ids = jnp.arange(slot_count, dtype=jnp.int32)
    live_slots = slot_ids[None, :] < counts_out[:, None]
    outgoing = jnp.where(live_slots[:, :, None], outgoing, jnp.zeros((), outgoing.dtype))
    payload = jnp.concatenate([outgoing, stripe_pieces], axis=1)
    arrived = lax.all_to_all(payload, AXES, split_axis=0, concat_axis=0, tiled=True)
    incoming_rows = arrived[:, :slot_count].reshape(peer_count * slot_count, feature_width)
    my_piece = jnp.sum(arrived[:, slot_count:].astype(jnp.float32), axis=0).astype(jnp.bfloat16)
    dense_bands = gather_pieces(my_piece, peer_count, group).reshape(
        stripe_count, tile_size, feature_width
    )

    dense_sum = jnp.zeros((block_count, tile_size, feature_width), jnp.float32)
    for tile_index in range(tiles_per):
        picked_tiles = dense_bands[dense_cols[:, tile_index]]
        dense_sum = dense_sum + jnp.einsum(
            "eim,emh->eih",
            dense_edge_weights[:, tile_index],
            picked_tiles,
            preferred_element_type=jnp.float32,
        )
    sparse_sum = jnp.dot(sparse_w, incoming_rows, preferred_element_type=jnp.float32)
    aggregate = (dense_sum.reshape(block_count * tile_size, feature_width) + sparse_sum).astype(
        jnp.bfloat16
    )
    result = jnp.dot(aggregate, weight, preferred_element_type=jnp.float32) + bias
    return jnp.maximum(result, 0.0).astype(jnp.bfloat16)


def solution(mesh):
    placed = (
        P(AXES, None),
        P(AXES, None, None, None),
        P(AXES, None),
        P(),
        P(AXES, None),
        P(AXES, None, None),
        P(AXES, None),
        P(),
        P(),
    )
    return jax.shard_map(
        on_device, mesh=mesh, in_specs=placed, out_specs=P(AXES, None), check_vma=False
    )
```

```python
import functools

import jax
import jax.numpy as jnp
from jax import lax
from jax.experimental import pallas as pl
from jax.experimental.pallas import tpu as pltpu
from jax.sharding import PartitionSpec as P

AXES = ("row", "grp")


def gather_kernel(group, piece_ref, out_ref, send_sem, recv_sem, local_sem):
    n = out_ref.shape[0]
    me = lax.axis_index(AXES)

    def where(peer):
        return (peer // group, peer % group)

    barrier = pltpu.get_barrier_semaphore()

    def greet(i, carry):
        peer = lax.rem(me + i, n)
        pl.semaphore_signal(barrier, inc=1, device_id=where(peer), device_id_type=pl.DeviceIdType.MESH)
        return carry

    lax.fori_loop(1, n, greet, 0)
    pl.semaphore_wait(barrier, n - 1)
    own = pltpu.make_async_copy(piece_ref, out_ref.at[me], local_sem)
    own.start()

    def send(i, carry):
        peer = lax.rem(me + i, n)
        pltpu.make_async_remote_copy(
            src_ref=piece_ref,
            dst_ref=out_ref.at[me],
            send_sem=send_sem.at[i],
            recv_sem=recv_sem.at[me],
            device_id=where(peer),
            device_id_type=pl.DeviceIdType.MESH,
        ).start()
        return carry

    lax.fori_loop(1, n, send, 0)

    def wait(i, carry):
        peer = lax.rem(me + i, n)
        source = lax.rem(me + n - i, n)
        pltpu.make_async_remote_copy(
            src_ref=piece_ref,
            dst_ref=out_ref.at[source],
            send_sem=send_sem.at[i],
            recv_sem=recv_sem.at[source],
            device_id=where(peer),
            device_id_type=pl.DeviceIdType.MESH,
        ).wait()
        return carry

    lax.fori_loop(1, n, wait, 0)
    own.wait()


def gather_pieces(piece, n, group):
    rows, width = piece.shape
    return pl.pallas_call(
        functools.partial(gather_kernel, group),
        out_shape=jax.ShapeDtypeStruct((n, rows, width), piece.dtype),
        in_specs=[pl.BlockSpec(memory_space=pltpu.VMEM)],
        out_specs=pl.BlockSpec(memory_space=pltpu.VMEM),
        scratch_shapes=[
            pltpu.SemaphoreType.DMA((n,)),
            pltpu.SemaphoreType.DMA((n,)),
            pltpu.SemaphoreType.DMA,
        ],
        compiler_params=pltpu.CompilerParams(collective_id=0, has_side_effects=True),
    )(piece)


def layer_kernel(tiles_per, cols_ref, w_ref, bands_ref, sw_ref, inc_ref, weight_ref, bias_ref, out_ref):
    block = pl.program_id(0)
    total = jnp.dot(sw_ref[...], inc_ref[...], preferred_element_type=jnp.float32)
    for tile_index in range(tiles_per):
        col = cols_ref[block * tiles_per + tile_index]
        total = total + jnp.dot(w_ref[0, tile_index], bands_ref[col], preferred_element_type=jnp.float32)
    aggregate = total.astype(jnp.bfloat16)
    result = jnp.dot(aggregate, weight_ref[...], preferred_element_type=jnp.float32) + bias_ref[...]
    out_ref[...] = jnp.maximum(result, 0.0).astype(out_ref.dtype)


def fused_layer(dense_cols, dense_edge_weights, dense_bands, sparse_w, incoming_rows, weight, bias):
    block_count, tiles_per, tile_size, _ = dense_edge_weights.shape
    stripe_count, _, width = dense_bands.shape
    slots = incoming_rows.shape[0]
    out_width = weight.shape[1]
    grid_spec = pltpu.PrefetchScalarGridSpec(
        num_scalar_prefetch=1,
        grid=(block_count,),
        in_specs=[
            pl.BlockSpec((1, tiles_per, tile_size, tile_size), lambda b, cols: (b, 0, 0, 0)),
            pl.BlockSpec((stripe_count, tile_size, width), lambda b, cols: (0, 0, 0)),
            pl.BlockSpec((tile_size, slots), lambda b, cols: (b, 0)),
            pl.BlockSpec((slots, width), lambda b, cols: (0, 0)),
            pl.BlockSpec((width, out_width), lambda b, cols: (0, 0)),
            pl.BlockSpec((1, out_width), lambda b, cols: (0, 0)),
        ],
        out_specs=pl.BlockSpec((tile_size, out_width), lambda b, cols: (b, 0)),
    )
    return pl.pallas_call(
        functools.partial(layer_kernel, tiles_per),
        grid_spec=grid_spec,
        out_shape=jax.ShapeDtypeStruct((block_count * tile_size, out_width), jnp.bfloat16),
    )(dense_cols.reshape(-1), dense_edge_weights, dense_bands, sparse_w, incoming_rows, weight, bias.reshape(1, -1))


def on_device(
    features,
    dense_edge_weights,
    dense_cols,
    dense_ids,
    sparse_w,
    sparse_rows,
    sparse_counts,
    weight,
    bias,
):
    block_count = dense_edge_weights.shape[0]
    tiles_per = dense_edge_weights.shape[1]
    tile_size = dense_edge_weights.shape[2]
    feature_width = features.shape[1]
    stripe_count = dense_ids.shape[0]
    local_blocks = features.reshape(block_count, tile_size, feature_width)
    group = lax.axis_size("grp")

    rows_out = sparse_rows[0]
    counts_out = sparse_counts[0]
    peer_count = rows_out.shape[0]
    slot_count = rows_out.shape[1]
    piece = stripe_count * tile_size // peer_count
    me = lax.axis_index(AXES)

    owners = dense_ids // block_count
    mine = owners == me
    candidates = local_blocks[dense_ids % block_count]
    candidates = jnp.where(mine[:, None, None], candidates, jnp.zeros((), candidates.dtype))
    stripe_pieces = candidates.reshape(peer_count, piece, feature_width)

    outgoing = features[rows_out]
    slot_ids = jnp.arange(slot_count, dtype=jnp.int32)
    live_slots = slot_ids[None, :] < counts_out[:, None]
    outgoing = jnp.where(live_slots[:, :, None], outgoing, jnp.zeros((), outgoing.dtype))
    payload = jnp.concatenate([outgoing, stripe_pieces], axis=1)
    arrived = lax.all_to_all(payload, AXES, split_axis=0, concat_axis=0, tiled=True)
    incoming_rows = arrived[:, :slot_count].reshape(peer_count * slot_count, feature_width)
    my_piece = jnp.sum(arrived[:, slot_count:].astype(jnp.float32), axis=0).astype(jnp.bfloat16)
    dense_bands = gather_pieces(my_piece, peer_count, group).reshape(
        stripe_count, tile_size, feature_width
    )

    return fused_layer(dense_cols, dense_edge_weights, dense_bands, sparse_w, incoming_rows, weight, bias)


def solution(mesh):
    placed = (
        P(AXES, None),
        P(AXES, None, None, None),
        P(AXES, None),
        P(),
        P(AXES, None),
        P(AXES, None, None),
        P(AXES, None),
        P(),
        P(),
    )
    return jax.shard_map(
        on_device, mesh=mesh, in_specs=placed, out_specs=P(AXES, None), check_vma=False
    )
```

```python
import functools

import jax
import jax.numpy as jnp
from jax import lax
from jax.experimental import pallas as pl
from jax.experimental.pallas import tpu as pltpu
from jax.sharding import PartitionSpec as P

AXES = ("row", "grp")


def gather_kernel(group, piece_ref, out_ref, send_sem, relay_sem, recv_sem, local_sem):
    n = out_ref.shape[0]
    chips = n // 2
    me = lax.axis_index(AXES)
    core = (me // group) % 2
    my_chip = (me // (2 * group)) * group + me % group
    mesh_ids = pl.DeviceIdType.MESH

    def device(chip, which_core):
        return ((chip // group) * 2 + which_core) * group + chip % group

    def where(k):
        return (k // group, k % group)

    def remote(src, dst, send, recv, k):
        return pltpu.make_async_remote_copy(
            src_ref=src, dst_ref=dst, send_sem=send, recv_sem=recv,
            device_id=where(k), device_id_type=mesh_ids,
        )

    partner = device(my_chip, 1 - core)
    barrier = pltpu.get_barrier_semaphore()
    pl.semaphore_signal(barrier, inc=1, device_id=where(partner), device_id_type=mesh_ids)

    def greet(i, carry):
        peer = device(lax.rem(my_chip + i, chips), core)
        pl.semaphore_signal(barrier, inc=1, device_id=where(peer), device_id_type=mesh_ids)
        return carry

    lax.fori_loop(1, chips, greet, 0)
    pl.semaphore_wait(barrier, chips)
    own = pltpu.make_async_copy(piece_ref, out_ref.at[me], local_sem)
    own.start()
    remote(piece_ref, out_ref.at[me], send_sem.at[0], recv_sem.at[me], partner).start()

    def send(i, carry):
        peer = device(lax.rem(my_chip + i, chips), core)
        remote(piece_ref, out_ref.at[me], send_sem.at[i], recv_sem.at[me], peer).start()
        return carry

    lax.fori_loop(1, chips, send, 0)

    def relay(i, carry):
        source = device(lax.rem(my_chip + chips - i, chips), core)
        remote(piece_ref, out_ref.at[source], send_sem.at[i], recv_sem.at[source], source).wait_recv()
        remote(out_ref.at[source], out_ref.at[source], relay_sem.at[i], recv_sem.at[source], partner).start()
        return carry

    lax.fori_loop(1, chips, relay, 0)
    remote(piece_ref, out_ref.at[partner], send_sem.at[0], recv_sem.at[partner], partner).wait_recv()

    def take(i, carry):
        source = device(lax.rem(my_chip + chips - i, chips), 1 - core)
        remote(piece_ref, out_ref.at[source], send_sem.at[i], recv_sem.at[source], partner).wait_recv()
        return carry

    lax.fori_loop(1, chips, take, 0)
    remote(piece_ref, out_ref.at[me], send_sem.at[0], recv_sem.at[me], partner).wait_send()

    def drain(i, carry):
        peer = device(lax.rem(my_chip + i, chips), core)
        remote(piece_ref, out_ref.at[me], send_sem.at[i], recv_sem.at[me], peer).wait_send()
        source = device(lax.rem(my_chip + chips - i, chips), core)
        remote(out_ref.at[source], out_ref.at[source], relay_sem.at[i], recv_sem.at[source], partner).wait_send()
        return carry

    lax.fori_loop(1, chips, drain, 0)
    own.wait()


def gather_pieces(piece, n, group):
    rows, width = piece.shape
    return pl.pallas_call(
        functools.partial(gather_kernel, group),
        out_shape=jax.ShapeDtypeStruct((n, rows, width), piece.dtype),
        in_specs=[pl.BlockSpec(memory_space=pltpu.VMEM)],
        out_specs=pl.BlockSpec(memory_space=pltpu.VMEM),
        scratch_shapes=[
            pltpu.SemaphoreType.DMA((n // 2,)),
            pltpu.SemaphoreType.DMA((n // 2,)),
            pltpu.SemaphoreType.DMA((n,)),
            pltpu.SemaphoreType.DMA,
        ],
        compiler_params=pltpu.CompilerParams(collective_id=0, has_side_effects=True),
    )(piece)

def layer_kernel(tiles_per, cols_ref, w_ref, bands_ref, sw_ref, inc_ref, weight_ref, bias_ref, out_ref):
    block = pl.program_id(0)
    total = jnp.dot(sw_ref[...], inc_ref[...], preferred_element_type=jnp.float32)
    for tile_index in range(tiles_per):
        col = cols_ref[block * tiles_per + tile_index]
        total = total + jnp.dot(w_ref[0, tile_index], bands_ref[col], preferred_element_type=jnp.float32)
    aggregate = total.astype(jnp.bfloat16)
    result = jnp.dot(aggregate, weight_ref[...], preferred_element_type=jnp.float32) + bias_ref[...]
    out_ref[...] = jnp.maximum(result, 0.0).astype(out_ref.dtype)


def fused_layer(dense_cols, dense_edge_weights, dense_bands, sparse_w, incoming_rows, weight, bias):
    block_count, tiles_per, tile_size, _ = dense_edge_weights.shape
    stripe_count, _, width = dense_bands.shape
    slots = incoming_rows.shape[0]
    out_width = weight.shape[1]
    grid_spec = pltpu.PrefetchScalarGridSpec(
        num_scalar_prefetch=1,
        grid=(block_count,),
        in_specs=[
            pl.BlockSpec((1, tiles_per, tile_size, tile_size), lambda b, cols: (b, 0, 0, 0)),
            pl.BlockSpec((stripe_count, tile_size, width), lambda b, cols: (0, 0, 0)),
            pl.BlockSpec((tile_size, slots), lambda b, cols: (b, 0)),
            pl.BlockSpec((slots, width), lambda b, cols: (0, 0)),
            pl.BlockSpec((width, out_width), lambda b, cols: (0, 0)),
            pl.BlockSpec((1, out_width), lambda b, cols: (0, 0)),
        ],
        out_specs=pl.BlockSpec((tile_size, out_width), lambda b, cols: (b, 0)),
    )
    return pl.pallas_call(
        functools.partial(layer_kernel, tiles_per),
        grid_spec=grid_spec,
        out_shape=jax.ShapeDtypeStruct((block_count * tile_size, out_width), jnp.bfloat16),
    )(dense_cols.reshape(-1), dense_edge_weights, dense_bands, sparse_w, incoming_rows, weight, bias.reshape(1, -1))


def on_device(
    features,
    dense_edge_weights,
    dense_cols,
    dense_ids,
    sparse_w,
    sparse_rows,
    sparse_counts,
    weight,
    bias,
):
    block_count = dense_edge_weights.shape[0]
    tiles_per = dense_edge_weights.shape[1]
    tile_size = dense_edge_weights.shape[2]
    feature_width = features.shape[1]
    stripe_count = dense_ids.shape[0]
    local_blocks = features.reshape(block_count, tile_size, feature_width)
    group = lax.axis_size("grp")

    rows_out = sparse_rows[0]
    counts_out = sparse_counts[0]
    peer_count = rows_out.shape[0]
    slot_count = rows_out.shape[1]
    piece = stripe_count * tile_size // peer_count
    me = lax.axis_index(AXES)

    owners = dense_ids // block_count
    mine = owners == me
    candidates = local_blocks[dense_ids % block_count]
    candidates = jnp.where(mine[:, None, None], candidates, jnp.zeros((), candidates.dtype))
    stripe_pieces = candidates.reshape(peer_count, piece, feature_width)

    outgoing = features[rows_out]
    slot_ids = jnp.arange(slot_count, dtype=jnp.int32)
    live_slots = slot_ids[None, :] < counts_out[:, None]
    outgoing = jnp.where(live_slots[:, :, None], outgoing, jnp.zeros((), outgoing.dtype))
    payload = jnp.concatenate([outgoing, stripe_pieces], axis=1)
    arrived = lax.all_to_all(payload, AXES, split_axis=0, concat_axis=0, tiled=True)
    incoming_rows = arrived[:, :slot_count].reshape(peer_count * slot_count, feature_width)
    my_piece = jnp.sum(arrived[:, slot_count:].astype(jnp.float32), axis=0).astype(jnp.bfloat16)
    dense_bands = gather_pieces(my_piece, peer_count, group).reshape(
        stripe_count, tile_size, feature_width
    )

    return fused_layer(dense_cols, dense_edge_weights, dense_bands, sparse_w, incoming_rows, weight, bias)


def solution(mesh):
    placed = (
        P(AXES, None),
        P(AXES, None, None, None),
        P(AXES, None),
        P(),
        P(AXES, None),
        P(AXES, None, None),
        P(AXES, None),
        P(),
        P(),
    )
    return jax.shard_map(
        on_device, mesh=mesh, in_specs=placed, out_specs=P(AXES, None), check_vma=False
    )
```

```python
import functools

import jax
import jax.numpy as jnp
from jax import lax
from jax.experimental import pallas as pl
from jax.experimental.pallas import tpu as pltpu
from jax.sharding import PartitionSpec as P

AXES = ("row", "grp")


def gather_kernel(group, piece_ref, out_ref, send_sem, relay_sem, recv_sem, local_sem):
    n = out_ref.shape[0]
    chips = n // 2
    me = lax.axis_index(AXES)
    core = (me // group) % 2
    my_chip = (me // (2 * group)) * group + me % group
    mesh_ids = pl.DeviceIdType.MESH

    def device(chip, which_core):
        return ((chip // group) * 2 + which_core) * group + chip % group

    def where(k):
        return (k // group, k % group)

    def remote(src, dst, send, recv, k):
        return pltpu.make_async_remote_copy(
            src_ref=src, dst_ref=dst, send_sem=send, recv_sem=recv,
            device_id=where(k), device_id_type=mesh_ids,
        )

    partner = device(my_chip, 1 - core)
    barrier = pltpu.get_barrier_semaphore()
    pl.semaphore_signal(barrier, inc=1, device_id=where(partner), device_id_type=mesh_ids)

    def greet(i, carry):
        peer = device(lax.rem(my_chip + i, chips), core)
        pl.semaphore_signal(barrier, inc=1, device_id=where(peer), device_id_type=mesh_ids)
        return carry

    lax.fori_loop(1, chips, greet, 0)
    pl.semaphore_wait(barrier, chips)
    own = pltpu.make_async_copy(piece_ref, out_ref.at[me], local_sem)
    own.start()
    remote(piece_ref, out_ref.at[me], send_sem.at[0], recv_sem.at[me], partner).start()

    def send(i, carry):
        peer = device(lax.rem(my_chip + i, chips), core)
        remote(piece_ref, out_ref.at[me], send_sem.at[i], recv_sem.at[me], peer).start()
        return carry

    lax.fori_loop(1, chips, send, 0)

    def relay(i, carry):
        source = device(lax.rem(my_chip + chips - i, chips), core)
        remote(piece_ref, out_ref.at[source], send_sem.at[i], recv_sem.at[source], source).wait_recv()
        remote(out_ref.at[source], out_ref.at[source], relay_sem.at[i], recv_sem.at[source], partner).start()
        return carry

    lax.fori_loop(1, chips, relay, 0)
    remote(piece_ref, out_ref.at[partner], send_sem.at[0], recv_sem.at[partner], partner).wait_recv()

    def take(i, carry):
        source = device(lax.rem(my_chip + chips - i, chips), 1 - core)
        remote(piece_ref, out_ref.at[source], send_sem.at[i], recv_sem.at[source], partner).wait_recv()
        return carry

    lax.fori_loop(1, chips, take, 0)
    remote(piece_ref, out_ref.at[me], send_sem.at[0], recv_sem.at[me], partner).wait_send()

    def drain(i, carry):
        peer = device(lax.rem(my_chip + i, chips), core)
        remote(piece_ref, out_ref.at[me], send_sem.at[i], recv_sem.at[me], peer).wait_send()
        source = device(lax.rem(my_chip + chips - i, chips), core)
        remote(out_ref.at[source], out_ref.at[source], relay_sem.at[i], recv_sem.at[source], partner).wait_send()
        return carry

    lax.fori_loop(1, chips, drain, 0)
    own.wait()


def gather_pieces(piece, n, group):
    rows, width = piece.shape
    return pl.pallas_call(
        functools.partial(gather_kernel, group),
        out_shape=jax.ShapeDtypeStruct((n, rows, width), piece.dtype),
        in_specs=[pl.BlockSpec(memory_space=pltpu.VMEM)],
        out_specs=pl.BlockSpec(memory_space=pltpu.VMEM),
        scratch_shapes=[
            pltpu.SemaphoreType.DMA((n // 2,)),
            pltpu.SemaphoreType.DMA((n // 2,)),
            pltpu.SemaphoreType.DMA((n,)),
            pltpu.SemaphoreType.DMA,
        ],
        compiler_params=pltpu.CompilerParams(collective_id=0, has_side_effects=True),
    )(piece)

def layer_kernel(tiles_per, cols_ref, w_ref, bands_ref, sw_ref, inc_ref, weight_ref, bias_ref, out_ref):
    block = pl.program_id(0)
    total = jnp.dot(sw_ref[...], inc_ref[...], preferred_element_type=jnp.float32)
    for tile_index in range(tiles_per):
        col = cols_ref[block * tiles_per + tile_index]
        total = total + jnp.dot(w_ref[0, tile_index], bands_ref[col], preferred_element_type=jnp.float32)
    aggregate = total.astype(jnp.bfloat16)
    result = jnp.dot(aggregate, weight_ref[...], preferred_element_type=jnp.float32) + bias_ref[...]
    out_ref[...] = jnp.maximum(result, 0.0).astype(out_ref.dtype)


def fused_layer(dense_cols, dense_edge_weights, dense_bands, sparse_w, incoming_rows, weight, bias):
    block_count, tiles_per, tile_size, _ = dense_edge_weights.shape
    stripe_count, _, width = dense_bands.shape
    slots = incoming_rows.shape[0]
    out_width = weight.shape[1]
    grid_spec = pltpu.PrefetchScalarGridSpec(
        num_scalar_prefetch=1,
        grid=(block_count,),
        in_specs=[
            pl.BlockSpec((1, tiles_per, tile_size, tile_size), lambda b, cols: (b, 0, 0, 0)),
            pl.BlockSpec((stripe_count, tile_size, width), lambda b, cols: (0, 0, 0)),
            pl.BlockSpec((tile_size, slots), lambda b, cols: (b, 0)),
            pl.BlockSpec((slots, width), lambda b, cols: (0, 0)),
            pl.BlockSpec((width, out_width), lambda b, cols: (0, 0)),
            pl.BlockSpec((1, out_width), lambda b, cols: (0, 0)),
        ],
        out_specs=pl.BlockSpec((tile_size, out_width), lambda b, cols: (b, 0)),
    )
    return pl.pallas_call(
        functools.partial(layer_kernel, tiles_per),
        grid_spec=grid_spec,
        out_shape=jax.ShapeDtypeStruct((block_count * tile_size, out_width), jnp.bfloat16),
    )(dense_cols.reshape(-1), dense_edge_weights, dense_bands, sparse_w, incoming_rows, weight, bias.reshape(1, -1))


def on_device(
    features,
    dense_edge_weights,
    dense_cols,
    dense_ids,
    sparse_w,
    sparse_rows,
    sparse_counts,
    weight,
    bias,
):
    block_count = dense_edge_weights.shape[0]
    tiles_per = dense_edge_weights.shape[1]
    tile_size = dense_edge_weights.shape[2]
    feature_width = features.shape[1]
    stripe_count = dense_ids.shape[0]
    local_blocks = features.reshape(block_count, tile_size, feature_width)
    group = lax.axis_size("grp")

    rows_out = sparse_rows[0]
    counts_out = sparse_counts[0]
    peer_count = rows_out.shape[0]
    slot_count = rows_out.shape[1]
    piece = stripe_count * tile_size // peer_count
    me = lax.axis_index(AXES)

    candidates = local_blocks[dense_ids % block_count]
    stripe_pieces = candidates.reshape(peer_count, piece, feature_width)

    outgoing = features[rows_out]
    slot_ids = jnp.arange(slot_count, dtype=jnp.int32)
    live_slots = slot_ids[None, :] < counts_out[:, None]
    outgoing = jnp.where(live_slots[:, :, None], outgoing, jnp.zeros((), outgoing.dtype))
    payload = jnp.concatenate([outgoing, stripe_pieces], axis=1)
    arrived = lax.all_to_all(payload, AXES, split_axis=0, concat_axis=0, tiled=True)
    incoming_rows = arrived[:, :slot_count].reshape(peer_count * slot_count, feature_width)
    my_owner = dense_ids[me * piece // tile_size] // block_count
    my_piece = lax.dynamic_index_in_dim(arrived, my_owner, 0, keepdims=False)[slot_count:]
    dense_bands = gather_pieces(my_piece, peer_count, group).reshape(
        stripe_count, tile_size, feature_width
    )

    return fused_layer(dense_cols, dense_edge_weights, dense_bands, sparse_w, incoming_rows, weight, bias)


def solution(mesh):
    placed = (
        P(AXES, None),
        P(AXES, None, None, None),
        P(AXES, None),
        P(),
        P(AXES, None),
        P(AXES, None, None),
        P(AXES, None),
        P(),
        P(),
    )
    return jax.shard_map(
        on_device, mesh=mesh, in_specs=placed, out_specs=P(AXES, None), check_vma=False
    )
```

```python
import functools

import jax
import jax.numpy as jnp
from jax import lax
from jax.experimental import pallas as pl
from jax.experimental.pallas import tpu as pltpu
from jax.sharding import PartitionSpec as P

AXES = ("row", "grp")


def gather_kernel(group, piece_ref, out_ref, send_sem, relay_sem, recv_sem, local_sem):
    n = out_ref.shape[0]
    chips = n // 2
    me = lax.axis_index(AXES)
    core = (me // group) % 2
    my_chip = (me // (2 * group)) * group + me % group
    mesh_ids = pl.DeviceIdType.MESH

    def device(chip, which_core):
        return ((chip // group) * 2 + which_core) * group + chip % group

    def where(k):
        return (k // group, k % group)

    def remote(src, dst, send, recv, k):
        return pltpu.make_async_remote_copy(
            src_ref=src, dst_ref=dst, send_sem=send, recv_sem=recv,
            device_id=where(k), device_id_type=mesh_ids,
        )

    partner = device(my_chip, 1 - core)
    barrier = pltpu.get_barrier_semaphore()
    pl.semaphore_signal(barrier, inc=1, device_id=where(partner), device_id_type=mesh_ids)

    def greet(i, carry):
        peer = device(lax.rem(my_chip + i, chips), core)
        pl.semaphore_signal(barrier, inc=1, device_id=where(peer), device_id_type=mesh_ids)
        return carry

    lax.fori_loop(1, chips, greet, 0)
    pl.semaphore_wait(barrier, chips)
    own = pltpu.make_async_copy(piece_ref, out_ref.at[me], local_sem)
    own.start()
    remote(piece_ref, out_ref.at[me], send_sem.at[0], recv_sem.at[me], partner).start()

    def send(i, carry):
        peer = device(lax.rem(my_chip + i, chips), core)
        remote(piece_ref, out_ref.at[me], send_sem.at[i], recv_sem.at[me], peer).start()
        return carry

    lax.fori_loop(1, chips, send, 0)

    def relay(i, carry):
        source = device(lax.rem(my_chip + chips - i, chips), core)
        remote(piece_ref, out_ref.at[source], send_sem.at[i], recv_sem.at[source], source).wait_recv()
        remote(out_ref.at[source], out_ref.at[source], relay_sem.at[i], recv_sem.at[source], partner).start()
        return carry

    lax.fori_loop(1, chips, relay, 0)
    remote(piece_ref, out_ref.at[partner], send_sem.at[0], recv_sem.at[partner], partner).wait_recv()

    def take(i, carry):
        source = device(lax.rem(my_chip + chips - i, chips), 1 - core)
        remote(piece_ref, out_ref.at[source], send_sem.at[i], recv_sem.at[source], partner).wait_recv()
        return carry

    lax.fori_loop(1, chips, take, 0)
    remote(piece_ref, out_ref.at[me], send_sem.at[0], recv_sem.at[me], partner).wait_send()

    def drain(i, carry):
        peer = device(lax.rem(my_chip + i, chips), core)
        remote(piece_ref, out_ref.at[me], send_sem.at[i], recv_sem.at[me], peer).wait_send()
        source = device(lax.rem(my_chip + chips - i, chips), core)
        remote(out_ref.at[source], out_ref.at[source], relay_sem.at[i], recv_sem.at[source], partner).wait_send()
        return carry

    lax.fori_loop(1, chips, drain, 0)
    own.wait()


def gather_pieces(piece, n, group):
    rows, width = piece.shape
    return pl.pallas_call(
        functools.partial(gather_kernel, group),
        out_shape=jax.ShapeDtypeStruct((n, rows, width), piece.dtype),
        in_specs=[pl.BlockSpec(memory_space=pltpu.VMEM)],
        out_specs=pl.BlockSpec(memory_space=pltpu.VMEM),
        scratch_shapes=[
            pltpu.SemaphoreType.DMA((n // 2,)),
            pltpu.SemaphoreType.DMA((n // 2,)),
            pltpu.SemaphoreType.DMA((n,)),
            pltpu.SemaphoreType.DMA,
        ],
        compiler_params=pltpu.CompilerParams(collective_id=0, has_side_effects=True),
    )(piece)

def layer_kernel(tiles_per, cols_ref, w_ref, bands_ref, sw_ref, inc_ref, weight_ref, bias_ref, out_ref):
    block = pl.program_id(0)
    total = jnp.dot(sw_ref[...], inc_ref[...], preferred_element_type=jnp.float32)
    for tile_index in range(tiles_per):
        col = cols_ref[block * tiles_per + tile_index]
        total = total + jnp.dot(w_ref[0, tile_index], bands_ref[col], preferred_element_type=jnp.float32)
    aggregate = total.astype(jnp.bfloat16)
    result = jnp.dot(aggregate, weight_ref[...], preferred_element_type=jnp.float32) + bias_ref[...]
    out_ref[...] = jnp.maximum(result, 0.0).astype(out_ref.dtype)


def fused_layer(dense_cols, dense_edge_weights, dense_bands, sparse_w, incoming_rows, weight, bias):
    block_count, tiles_per, tile_size, _ = dense_edge_weights.shape
    stripe_count, _, width = dense_bands.shape
    slots = incoming_rows.shape[0]
    out_width = weight.shape[1]
    grid_spec = pltpu.PrefetchScalarGridSpec(
        num_scalar_prefetch=1,
        grid=(block_count,),
        in_specs=[
            pl.BlockSpec((1, tiles_per, tile_size, tile_size), lambda b, cols: (b, 0, 0, 0)),
            pl.BlockSpec((stripe_count, tile_size, width), lambda b, cols: (0, 0, 0)),
            pl.BlockSpec((tile_size, slots), lambda b, cols: (b, 0)),
            pl.BlockSpec((slots, width), lambda b, cols: (0, 0)),
            pl.BlockSpec((width, out_width), lambda b, cols: (0, 0)),
            pl.BlockSpec((1, out_width), lambda b, cols: (0, 0)),
        ],
        out_specs=pl.BlockSpec((tile_size, out_width), lambda b, cols: (b, 0)),
    )
    return pl.pallas_call(
        functools.partial(layer_kernel, tiles_per),
        grid_spec=grid_spec,
        out_shape=jax.ShapeDtypeStruct((block_count * tile_size, out_width), jnp.bfloat16),
    )(dense_cols.reshape(-1), dense_edge_weights, dense_bands, sparse_w, incoming_rows, weight, bias.reshape(1, -1))


def on_device(
    features,
    dense_edge_weights,
    dense_cols,
    dense_ids,
    sparse_w,
    sparse_rows,
    sparse_counts,
    weight,
    bias,
):
    block_count = dense_edge_weights.shape[0]
    tiles_per = dense_edge_weights.shape[1]
    tile_size = dense_edge_weights.shape[2]
    feature_width = features.shape[1]
    stripe_count = dense_ids.shape[0]
    local_blocks = features.reshape(block_count, tile_size, feature_width)
    group = lax.axis_size("grp")

    rows_out = sparse_rows[0]
    counts_out = sparse_counts[0]
    peer_count = rows_out.shape[0]
    slot_count = rows_out.shape[1]
    piece = stripe_count * tile_size // peer_count
    me = lax.axis_index(AXES)

    stripe_rows = jnp.arange(stripe_count * tile_size, dtype=jnp.int32)
    stripe_rows = (dense_ids % block_count)[stripe_rows // tile_size] * tile_size + stripe_rows % tile_size
    row_ids = jnp.concatenate([rows_out, stripe_rows.reshape(peer_count, piece)], axis=1)
    slot_ids = jnp.arange(slot_count + piece, dtype=jnp.int32)
    live_slots = (slot_ids[None, :] < counts_out[:, None]) | (slot_ids[None, :] >= slot_count)
    payload = jnp.where(live_slots[:, :, None], features[row_ids], jnp.zeros((), features.dtype))
    arrived = lax.all_to_all(payload, AXES, split_axis=0, concat_axis=0, tiled=True)
    incoming_rows = arrived[:, :slot_count].reshape(peer_count * slot_count, feature_width)
    my_owner = dense_ids[me * piece // tile_size] // block_count
    my_piece = lax.dynamic_index_in_dim(arrived, my_owner, 0, keepdims=False)[slot_count:]
    dense_bands = gather_pieces(my_piece, peer_count, group).reshape(
        stripe_count, tile_size, feature_width
    )

    return fused_layer(dense_cols, dense_edge_weights, dense_bands, sparse_w, incoming_rows, weight, bias)


def solution(mesh):
    placed = (
        P(AXES, None),
        P(AXES, None, None, None),
        P(AXES, None),
        P(),
        P(AXES, None),
        P(AXES, None, None),
        P(AXES, None),
        P(),
        P(),
    )
    return jax.shard_map(
        on_device, mesh=mesh, in_specs=placed, out_specs=P(AXES, None), check_vma=False
    )
```

```python
import functools

import jax
import jax.numpy as jnp
from jax import lax
from jax.experimental import pallas as pl
from jax.experimental.pallas import tpu as pltpu
from jax.sharding import PartitionSpec as P

AXES = ("row", "grp")


def gather_kernel(group, piece_ref, out_ref, send_sem, relay_sem, recv_sem, local_sem):
    n = out_ref.shape[0]
    chips = n // 2
    me = lax.axis_index(AXES)
    core = (me // group) % 2
    my_chip = (me // (2 * group)) * group + me % group
    mesh_ids = pl.DeviceIdType.MESH

    def device(chip, which_core):
        return ((chip // group) * 2 + which_core) * group + chip % group

    def where(k):
        return (k // group, k % group)

    def remote(src, dst, send, recv, k):
        return pltpu.make_async_remote_copy(
            src_ref=src, dst_ref=dst, send_sem=send, recv_sem=recv,
            device_id=where(k), device_id_type=mesh_ids,
        )

    partner = device(my_chip, 1 - core)
    barrier = pltpu.get_barrier_semaphore()
    pl.semaphore_signal(barrier, inc=1, device_id=where(partner), device_id_type=mesh_ids)

    def greet(i, carry):
        peer = device(lax.rem(my_chip + i, chips), core)
        pl.semaphore_signal(barrier, inc=1, device_id=where(peer), device_id_type=mesh_ids)
        return carry

    lax.fori_loop(1, chips, greet, 0)
    pl.semaphore_wait(barrier, chips)
    own = pltpu.make_async_copy(piece_ref, out_ref.at[me], local_sem)
    own.start()
    remote(piece_ref, out_ref.at[me], send_sem.at[0], recv_sem.at[me], partner).start()

    def send(i, carry):
        peer = device(lax.rem(my_chip + i, chips), core)
        remote(piece_ref, out_ref.at[me], send_sem.at[i], recv_sem.at[me], peer).start()
        return carry

    lax.fori_loop(1, chips, send, 0)

    def relay(i, carry):
        source = device(lax.rem(my_chip + chips - i, chips), core)
        remote(piece_ref, out_ref.at[source], send_sem.at[i], recv_sem.at[source], source).wait_recv()
        remote(out_ref.at[source], out_ref.at[source], relay_sem.at[i], recv_sem.at[source], partner).start()
        return carry

    lax.fori_loop(1, chips, relay, 0)
    remote(piece_ref, out_ref.at[partner], send_sem.at[0], recv_sem.at[partner], partner).wait_recv()

    def take(i, carry):
        source = device(lax.rem(my_chip + chips - i, chips), 1 - core)
        remote(piece_ref, out_ref.at[source], send_sem.at[i], recv_sem.at[source], partner).wait_recv()
        return carry

    lax.fori_loop(1, chips, take, 0)
    remote(piece_ref, out_ref.at[me], send_sem.at[0], recv_sem.at[me], partner).wait_send()

    def drain(i, carry):
        peer = device(lax.rem(my_chip + i, chips), core)
        remote(piece_ref, out_ref.at[me], send_sem.at[i], recv_sem.at[me], peer).wait_send()
        source = device(lax.rem(my_chip + chips - i, chips), core)
        remote(out_ref.at[source], out_ref.at[source], relay_sem.at[i], recv_sem.at[source], partner).wait_send()
        return carry

    lax.fori_loop(1, chips, drain, 0)
    own.wait()


def gather_pieces(piece, n, group):
    rows, width = piece.shape
    return pl.pallas_call(
        functools.partial(gather_kernel, group),
        out_shape=jax.ShapeDtypeStruct((n, rows, width), piece.dtype),
        in_specs=[pl.BlockSpec(memory_space=pltpu.VMEM)],
        out_specs=pl.BlockSpec(memory_space=pltpu.VMEM),
        scratch_shapes=[
            pltpu.SemaphoreType.DMA((n // 2,)),
            pltpu.SemaphoreType.DMA((n // 2,)),
            pltpu.SemaphoreType.DMA((n,)),
            pltpu.SemaphoreType.DMA,
        ],
        compiler_params=pltpu.CompilerParams(collective_id=0, has_side_effects=True),
    )(piece)

def layer_kernel(tiles_per, cols_ref, w_ref, bands_ref, sw_ref, inc_ref, weight_ref, bias_ref, out_ref):
    block = pl.program_id(0)
    total = jnp.dot(sw_ref[...], inc_ref[...], preferred_element_type=jnp.float32)
    for tile_index in range(tiles_per):
        col = cols_ref[block * tiles_per + tile_index]
        total = total + jnp.dot(w_ref[0, tile_index], bands_ref[col], preferred_element_type=jnp.float32)
    aggregate = total.astype(jnp.bfloat16)
    result = jnp.dot(aggregate, weight_ref[...], preferred_element_type=jnp.float32) + bias_ref[...]
    out_ref[...] = jnp.maximum(result, 0.0).astype(out_ref.dtype)


def fused_layer(dense_cols, dense_edge_weights, dense_bands, sparse_w, incoming_rows, weight, bias):
    block_count, tiles_per, tile_size, _ = dense_edge_weights.shape
    stripe_count, _, width = dense_bands.shape
    slots = incoming_rows.shape[0]
    out_width = weight.shape[1]
    grid_spec = pltpu.PrefetchScalarGridSpec(
        num_scalar_prefetch=1,
        grid=(block_count,),
        in_specs=[
            pl.BlockSpec((1, tiles_per, tile_size, tile_size), lambda b, cols: (b, 0, 0, 0)),
            pl.BlockSpec((stripe_count, tile_size, width), lambda b, cols: (0, 0, 0)),
            pl.BlockSpec((tile_size, slots), lambda b, cols: (b, 0)),
            pl.BlockSpec((slots, width), lambda b, cols: (0, 0)),
            pl.BlockSpec((width, out_width), lambda b, cols: (0, 0)),
            pl.BlockSpec((1, out_width), lambda b, cols: (0, 0)),
        ],
        out_specs=pl.BlockSpec((tile_size, out_width), lambda b, cols: (b, 0)),
    )
    return pl.pallas_call(
        functools.partial(layer_kernel, tiles_per),
        grid_spec=grid_spec,
        out_shape=jax.ShapeDtypeStruct((block_count * tile_size, out_width), jnp.bfloat16),
    )(dense_cols.reshape(-1), dense_edge_weights, dense_bands, sparse_w, incoming_rows, weight, bias.reshape(1, -1))


def on_device(
    features,
    dense_edge_weights,
    dense_cols,
    dense_ids,
    sparse_w,
    sparse_rows,
    sparse_counts,
    weight,
    bias,
):
    block_count = dense_edge_weights.shape[0]
    tiles_per = dense_edge_weights.shape[1]
    tile_size = dense_edge_weights.shape[2]
    feature_width = features.shape[1]
    stripe_count = dense_ids.shape[0]
    local_blocks = features.reshape(block_count, tile_size, feature_width)
    group = lax.axis_size("grp")

    rows_out = sparse_rows[0]
    counts_out = sparse_counts[0]
    peer_count = rows_out.shape[0]
    slot_count = rows_out.shape[1]
    piece = stripe_count * tile_size // peer_count
    me = lax.axis_index(AXES)

    candidates = local_blocks[dense_ids % block_count]
    stripe_pieces = candidates.reshape(peer_count, piece, feature_width)

    stripe_arrived = lax.all_to_all(stripe_pieces, AXES, split_axis=0, concat_axis=0, tiled=True)
    my_owner = dense_ids[me * piece // tile_size] // block_count
    my_piece = lax.dynamic_index_in_dim(stripe_arrived, my_owner, 0, keepdims=False)

    outgoing = features[rows_out]
    slot_ids = jnp.arange(slot_count, dtype=jnp.int32)
    live_slots = slot_ids[None, :] < counts_out[:, None]
    outgoing = jnp.where(live_slots[:, :, None], outgoing, jnp.zeros((), outgoing.dtype))
    arrived = lax.all_to_all(outgoing, AXES, split_axis=0, concat_axis=0, tiled=True)
    incoming_rows = arrived.reshape(peer_count * slot_count, feature_width)
    dense_bands = gather_pieces(my_piece, peer_count, group).reshape(
        stripe_count, tile_size, feature_width
    )

    return fused_layer(dense_cols, dense_edge_weights, dense_bands, sparse_w, incoming_rows, weight, bias)


def solution(mesh):
    placed = (
        P(AXES, None),
        P(AXES, None, None, None),
        P(AXES, None),
        P(),
        P(AXES, None),
        P(AXES, None, None),
        P(AXES, None),
        P(),
        P(),
    )
    return jax.shard_map(
        on_device, mesh=mesh, in_specs=placed, out_specs=P(AXES, None), check_vma=False
    )
```

```python
import functools

import jax
import jax.numpy as jnp
from jax import lax
from jax.experimental import pallas as pl
from jax.experimental.pallas import tpu as pltpu
from jax.sharding import PartitionSpec as P

AXES = ("row", "grp")


def gather_kernel(group, piece_ref, out_ref, send_sem, relay_sem, recv_sem, local_sem):
    n = out_ref.shape[0]
    chips = n // 2
    me = lax.axis_index(AXES)
    core = (me // group) % 2
    my_chip = (me // (2 * group)) * group + me % group
    mesh_ids = pl.DeviceIdType.MESH

    def device(chip, which_core):
        return ((chip // group) * 2 + which_core) * group + chip % group

    def where(k):
        return (k // group, k % group)

    def remote(src, dst, send, recv, k):
        return pltpu.make_async_remote_copy(
            src_ref=src, dst_ref=dst, send_sem=send, recv_sem=recv,
            device_id=where(k), device_id_type=mesh_ids,
        )

    partner = device(my_chip, 1 - core)
    barrier = pltpu.get_barrier_semaphore()
    pl.semaphore_signal(barrier, inc=1, device_id=where(partner), device_id_type=mesh_ids)

    def greet(i, carry):
        peer = device(lax.rem(my_chip + i, chips), core)
        pl.semaphore_signal(barrier, inc=1, device_id=where(peer), device_id_type=mesh_ids)
        return carry

    lax.fori_loop(1, chips, greet, 0)
    pl.semaphore_wait(barrier, chips)
    own = pltpu.make_async_copy(piece_ref, out_ref.at[me], local_sem)
    own.start()
    remote(piece_ref, out_ref.at[me], send_sem.at[0], recv_sem.at[me], partner).start()

    def send(i, carry):
        peer = device(lax.rem(my_chip + i, chips), core)
        remote(piece_ref, out_ref.at[me], send_sem.at[i], recv_sem.at[me], peer).start()
        return carry

    lax.fori_loop(1, chips, send, 0)

    def relay(i, carry):
        source = device(lax.rem(my_chip + chips - i, chips), core)
        remote(piece_ref, out_ref.at[source], send_sem.at[i], recv_sem.at[source], source).wait_recv()
        remote(out_ref.at[source], out_ref.at[source], relay_sem.at[i], recv_sem.at[source], partner).start()
        return carry

    lax.fori_loop(1, chips, relay, 0)
    remote(piece_ref, out_ref.at[partner], send_sem.at[0], recv_sem.at[partner], partner).wait_recv()

    def take(i, carry):
        source = device(lax.rem(my_chip + chips - i, chips), 1 - core)
        remote(piece_ref, out_ref.at[source], send_sem.at[i], recv_sem.at[source], partner).wait_recv()
        return carry

    lax.fori_loop(1, chips, take, 0)
    remote(piece_ref, out_ref.at[me], send_sem.at[0], recv_sem.at[me], partner).wait_send()

    def drain(i, carry):
        peer = device(lax.rem(my_chip + i, chips), core)
        remote(piece_ref, out_ref.at[me], send_sem.at[i], recv_sem.at[me], peer).wait_send()
        source = device(lax.rem(my_chip + chips - i, chips), core)
        remote(out_ref.at[source], out_ref.at[source], relay_sem.at[i], recv_sem.at[source], partner).wait_send()
        return carry

    lax.fori_loop(1, chips, drain, 0)
    own.wait()


def gather_pieces(piece, n, group):
    rows, width = piece.shape
    return pl.pallas_call(
        functools.partial(gather_kernel, group),
        out_shape=jax.ShapeDtypeStruct((n, rows, width), piece.dtype),
        in_specs=[pl.BlockSpec(memory_space=pltpu.VMEM)],
        out_specs=pl.BlockSpec(memory_space=pltpu.VMEM),
        scratch_shapes=[
            pltpu.SemaphoreType.DMA((n // 2,)),
            pltpu.SemaphoreType.DMA((n // 2,)),
            pltpu.SemaphoreType.DMA((n,)),
            pltpu.SemaphoreType.DMA,
        ],
        compiler_params=pltpu.CompilerParams(collective_id=0, has_side_effects=True),
    )(piece)

def layer_kernel(tiles_per, tile_size, step_blocks, cols_ref, w_ref, bands_ref, sw_ref, inc_ref, weight_ref, bias_ref, out_ref):
    step = pl.program_id(0)
    for half in range(step_blocks):
        rows = pl.ds(half * tile_size, tile_size)
        total = jnp.dot(sw_ref[rows], inc_ref[...], preferred_element_type=jnp.float32)
        for tile_index in range(tiles_per):
            col = cols_ref[(step * step_blocks + half) * tiles_per + tile_index]
            total = total + jnp.dot(w_ref[half, tile_index], bands_ref[col], preferred_element_type=jnp.float32)
        aggregate = total.astype(jnp.bfloat16)
        result = jnp.dot(aggregate, weight_ref[...], preferred_element_type=jnp.float32) + bias_ref[...]
        out_ref[rows] = jnp.maximum(result, 0.0).astype(out_ref.dtype)


def fused_layer(dense_cols, dense_edge_weights, dense_bands, sparse_w, incoming_rows, weight, bias):
    block_count, tiles_per, tile_size, _ = dense_edge_weights.shape
    stripe_count, _, width = dense_bands.shape
    slots = incoming_rows.shape[0]
    out_width = weight.shape[1]
    step_blocks = 2 if block_count % 2 == 0 else 1
    grid_spec = pltpu.PrefetchScalarGridSpec(
        num_scalar_prefetch=1,
        grid=(block_count // step_blocks,),
        in_specs=[
            pl.BlockSpec((step_blocks, tiles_per, tile_size, tile_size), lambda b, cols: (b, 0, 0, 0)),
            pl.BlockSpec((stripe_count, tile_size, width), lambda b, cols: (0, 0, 0)),
            pl.BlockSpec((step_blocks * tile_size, slots), lambda b, cols: (b, 0)),
            pl.BlockSpec((slots, width), lambda b, cols: (0, 0)),
            pl.BlockSpec((width, out_width), lambda b, cols: (0, 0)),
            pl.BlockSpec((1, out_width), lambda b, cols: (0, 0)),
        ],
        out_specs=pl.BlockSpec((step_blocks * tile_size, out_width), lambda b, cols: (b, 0)),
    )
    return pl.pallas_call(
        functools.partial(layer_kernel, tiles_per, tile_size, step_blocks),
        grid_spec=grid_spec,
        out_shape=jax.ShapeDtypeStruct((block_count * tile_size, out_width), jnp.bfloat16),
    )(dense_cols.reshape(-1), dense_edge_weights, dense_bands, sparse_w, incoming_rows, weight, bias.reshape(1, -1))

def on_device(
    features,
    dense_edge_weights,
    dense_cols,
    dense_ids,
    sparse_w,
    sparse_rows,
    sparse_counts,
    weight,
    bias,
):
    block_count = dense_edge_weights.shape[0]
    tiles_per = dense_edge_weights.shape[1]
    tile_size = dense_edge_weights.shape[2]
    feature_width = features.shape[1]
    stripe_count = dense_ids.shape[0]
    local_blocks = features.reshape(block_count, tile_size, feature_width)
    group = lax.axis_size("grp")

    rows_out = sparse_rows[0]
    counts_out = sparse_counts[0]
    peer_count = rows_out.shape[0]
    slot_count = rows_out.shape[1]
    piece = stripe_count * tile_size // peer_count
    me = lax.axis_index(AXES)

    candidates = local_blocks[dense_ids % block_count]
    stripe_pieces = candidates.reshape(peer_count, piece, feature_width)

    stripe_arrived = lax.all_to_all(stripe_pieces, AXES, split_axis=0, concat_axis=0, tiled=True)
    my_owner = dense_ids[me * piece // tile_size] // block_count
    my_piece = lax.dynamic_index_in_dim(stripe_arrived, my_owner, 0, keepdims=False)

    outgoing = features[rows_out]
    slot_ids = jnp.arange(slot_count, dtype=jnp.int32)
    live_slots = slot_ids[None, :] < counts_out[:, None]
    outgoing = jnp.where(live_slots[:, :, None], outgoing, jnp.zeros((), outgoing.dtype))
    arrived = lax.all_to_all(outgoing, AXES, split_axis=0, concat_axis=0, tiled=True)
    incoming_rows = arrived.reshape(peer_count * slot_count, feature_width)
    dense_bands = gather_pieces(my_piece, peer_count, group).reshape(
        stripe_count, tile_size, feature_width
    )

    return fused_layer(dense_cols, dense_edge_weights, dense_bands, sparse_w, incoming_rows, weight, bias)


def solution(mesh):
    placed = (
        P(AXES, None),
        P(AXES, None, None, None),
        P(AXES, None),
        P(),
        P(AXES, None),
        P(AXES, None, None),
        P(AXES, None),
        P(),
        P(),
    )
    return jax.shard_map(
        on_device, mesh=mesh, in_specs=placed, out_specs=P(AXES, None), check_vma=False
    )
```

```python
import functools

import jax
import jax.numpy as jnp
from jax import lax
from jax.experimental import pallas as pl
from jax.experimental.pallas import tpu as pltpu
from jax.sharding import PartitionSpec as P

AXES = ("row", "grp")


def gather_kernel(group, piece_ref, out_ref, send_sem, relay_sem, recv_sem, local_sem):
    n = out_ref.shape[0]
    chips = n // 2
    me = lax.axis_index(AXES)
    core = (me // group) % 2
    my_chip = (me // (2 * group)) * group + me % group
    mesh_ids = pl.DeviceIdType.MESH

    def device(chip, which_core):
        return ((chip // group) * 2 + which_core) * group + chip % group

    def where(k):
        return (k // group, k % group)

    def remote(src, dst, send, recv, k):
        return pltpu.make_async_remote_copy(
            src_ref=src, dst_ref=dst, send_sem=send, recv_sem=recv,
            device_id=where(k), device_id_type=mesh_ids,
        )

    partner = device(my_chip, 1 - core)
    barrier = pltpu.get_barrier_semaphore()
    pl.semaphore_signal(barrier, inc=1, device_id=where(partner), device_id_type=mesh_ids)

    def greet(i, carry):
        peer = device(lax.rem(my_chip + i, chips), core)
        pl.semaphore_signal(barrier, inc=1, device_id=where(peer), device_id_type=mesh_ids)
        return carry

    lax.fori_loop(1, chips, greet, 0)
    pl.semaphore_wait(barrier, chips)
    own = pltpu.make_async_copy(piece_ref, out_ref.at[me], local_sem)
    own.start()
    remote(piece_ref, out_ref.at[me], send_sem.at[0], recv_sem.at[me], partner).start()

    def send(i, carry):
        peer = device(lax.rem(my_chip + i, chips), core)
        remote(piece_ref, out_ref.at[me], send_sem.at[i], recv_sem.at[me], peer).start()
        return carry

    lax.fori_loop(1, chips, send, 0)

    def relay(i, carry):
        source = device(lax.rem(my_chip + chips - i, chips), core)
        remote(piece_ref, out_ref.at[source], send_sem.at[i], recv_sem.at[source], source).wait_recv()
        remote(out_ref.at[source], out_ref.at[source], relay_sem.at[i], recv_sem.at[source], partner).start()
        return carry

    lax.fori_loop(1, chips, relay, 0)
    remote(piece_ref, out_ref.at[partner], send_sem.at[0], recv_sem.at[partner], partner).wait_recv()

    def take(i, carry):
        source = device(lax.rem(my_chip + chips - i, chips), 1 - core)
        remote(piece_ref, out_ref.at[source], send_sem.at[i], recv_sem.at[source], partner).wait_recv()
        return carry

    lax.fori_loop(1, chips, take, 0)
    remote(piece_ref, out_ref.at[me], send_sem.at[0], recv_sem.at[me], partner).wait_send()

    def drain(i, carry):
        peer = device(lax.rem(my_chip + i, chips), core)
        remote(piece_ref, out_ref.at[me], send_sem.at[i], recv_sem.at[me], peer).wait_send()
        source = device(lax.rem(my_chip + chips - i, chips), core)
        remote(out_ref.at[source], out_ref.at[source], relay_sem.at[i], recv_sem.at[source], partner).wait_send()
        return carry

    lax.fori_loop(1, chips, drain, 0)
    own.wait()


def gather_pieces(piece, n, group):
    rows, width = piece.shape
    return pl.pallas_call(
        functools.partial(gather_kernel, group),
        out_shape=jax.ShapeDtypeStruct((n, rows, width), piece.dtype),
        in_specs=[pl.BlockSpec(memory_space=pltpu.VMEM)],
        out_specs=pl.BlockSpec(memory_space=pltpu.VMEM),
        scratch_shapes=[
            pltpu.SemaphoreType.DMA((n // 2,)),
            pltpu.SemaphoreType.DMA((n // 2,)),
            pltpu.SemaphoreType.DMA((n,)),
            pltpu.SemaphoreType.DMA,
        ],
        compiler_params=pltpu.CompilerParams(collective_id=0, has_side_effects=True),
    )(piece)

def exchange_kernel(group, pay_ref, out_ref, send_sem, recv_sem, local_sem):
    n = out_ref.shape[0]
    me = lax.axis_index(AXES)
    mesh_ids = pl.DeviceIdType.MESH

    def where(k):
        return (k // group, k % group)

    barrier = pltpu.get_barrier_semaphore()

    def greet(i, carry):
        peer = lax.rem(me + i, n)
        pl.semaphore_signal(barrier, inc=1, device_id=where(peer), device_id_type=mesh_ids)
        return carry

    lax.fori_loop(1, n, greet, 0)
    pl.semaphore_wait(barrier, n - 1)
    own = pltpu.make_async_copy(pay_ref.at[me], out_ref.at[me], local_sem)
    own.start()

    def send(i, carry):
        peer = lax.rem(me + i, n)
        pltpu.make_async_remote_copy(
            src_ref=pay_ref.at[peer], dst_ref=out_ref.at[me], send_sem=send_sem.at[i],
            recv_sem=recv_sem.at[me], device_id=where(peer), device_id_type=mesh_ids,
        ).start()
        return carry

    lax.fori_loop(1, n, send, 0)

    def wait(i, carry):
        peer = lax.rem(me + i, n)
        source = lax.rem(me + n - i, n)
        pltpu.make_async_remote_copy(
            src_ref=pay_ref.at[peer], dst_ref=out_ref.at[source], send_sem=send_sem.at[i],
            recv_sem=recv_sem.at[source], device_id=where(peer), device_id_type=mesh_ids,
        ).wait()
        return carry

    lax.fori_loop(1, n, wait, 0)
    own.wait()


def exchange_rows(payload, group):
    n = payload.shape[0]
    return pl.pallas_call(
        functools.partial(exchange_kernel, group),
        out_shape=jax.ShapeDtypeStruct(payload.shape, payload.dtype),
        in_specs=[pl.BlockSpec(memory_space=pltpu.VMEM)],
        out_specs=pl.BlockSpec(memory_space=pltpu.VMEM),
        scratch_shapes=[
            pltpu.SemaphoreType.DMA((n,)),
            pltpu.SemaphoreType.DMA((n,)),
            pltpu.SemaphoreType.DMA,
        ],
        cost_estimate=pl.CostEstimate(flops=0, transcendentals=0, bytes_accessed=2 * payload.size * payload.dtype.itemsize),
        compiler_params=pltpu.CompilerParams(collective_id=1, has_side_effects=True),
    )(payload)


def layer_kernel(tiles_per, tile_size, step_blocks, cols_ref, w_ref, bands_ref, sw_ref, inc_ref, weight_ref, bias_ref, out_ref):
    step = pl.program_id(0)
    for half in range(step_blocks):
        rows = pl.ds(half * tile_size, tile_size)
        total = jnp.dot(sw_ref[rows], inc_ref[...], preferred_element_type=jnp.float32)
        for tile_index in range(tiles_per):
            col = cols_ref[(step * step_blocks + half) * tiles_per + tile_index]
            total = total + jnp.dot(w_ref[half, tile_index], bands_ref[col], preferred_element_type=jnp.float32)
        aggregate = total.astype(jnp.bfloat16)
        result = jnp.dot(aggregate, weight_ref[...], preferred_element_type=jnp.float32) + bias_ref[...]
        out_ref[rows] = jnp.maximum(result, 0.0).astype(out_ref.dtype)


def fused_layer(dense_cols, dense_edge_weights, dense_bands, sparse_w, incoming_rows, weight, bias):
    block_count, tiles_per, tile_size, _ = dense_edge_weights.shape
    stripe_count, _, width = dense_bands.shape
    slots = incoming_rows.shape[0]
    out_width = weight.shape[1]
    step_blocks = 2 if block_count % 2 == 0 else 1
    grid_spec = pltpu.PrefetchScalarGridSpec(
        num_scalar_prefetch=1,
        grid=(block_count // step_blocks,),
        in_specs=[
            pl.BlockSpec((step_blocks, tiles_per, tile_size, tile_size), lambda b, cols: (b, 0, 0, 0)),
            pl.BlockSpec((stripe_count, tile_size, width), lambda b, cols: (0, 0, 0)),
            pl.BlockSpec((step_blocks * tile_size, slots), lambda b, cols: (b, 0)),
            pl.BlockSpec((slots, width), lambda b, cols: (0, 0)),
            pl.BlockSpec((width, out_width), lambda b, cols: (0, 0)),
            pl.BlockSpec((1, out_width), lambda b, cols: (0, 0)),
        ],
        out_specs=pl.BlockSpec((step_blocks * tile_size, out_width), lambda b, cols: (b, 0)),
    )
    return pl.pallas_call(
        functools.partial(layer_kernel, tiles_per, tile_size, step_blocks),
        grid_spec=grid_spec,
        out_shape=jax.ShapeDtypeStruct((block_count * tile_size, out_width), jnp.bfloat16),
    )(dense_cols.reshape(-1), dense_edge_weights, dense_bands, sparse_w, incoming_rows, weight, bias.reshape(1, -1))

def on_device(
    features,
    dense_edge_weights,
    dense_cols,
    dense_ids,
    sparse_w,
    sparse_rows,
    sparse_counts,
    weight,
    bias,
):
    block_count = dense_edge_weights.shape[0]
    tiles_per = dense_edge_weights.shape[1]
    tile_size = dense_edge_weights.shape[2]
    feature_width = features.shape[1]
    stripe_count = dense_ids.shape[0]
    local_blocks = features.reshape(block_count, tile_size, feature_width)
    group = lax.axis_size("grp")

    rows_out = sparse_rows[0]
    counts_out = sparse_counts[0]
    peer_count = rows_out.shape[0]
    slot_count = rows_out.shape[1]
    piece = stripe_count * tile_size // peer_count
    me = lax.axis_index(AXES)

    candidates = local_blocks[dense_ids % block_count]
    stripe_pieces = candidates.reshape(peer_count, piece, feature_width)

    stripe_arrived = lax.all_to_all(stripe_pieces, AXES, split_axis=0, concat_axis=0, tiled=True)
    my_owner = dense_ids[me * piece // tile_size] // block_count
    my_piece = lax.dynamic_index_in_dim(stripe_arrived, my_owner, 0, keepdims=False)

    outgoing = features[rows_out]
    slot_ids = jnp.arange(slot_count, dtype=jnp.int32)
    live_slots = slot_ids[None, :] < counts_out[:, None]
    outgoing = jnp.where(live_slots[:, :, None], outgoing, jnp.zeros((), outgoing.dtype))
    arrived = exchange_rows(outgoing, group)
    incoming_rows = arrived.reshape(peer_count * slot_count, feature_width)
    dense_bands = gather_pieces(my_piece, peer_count, group).reshape(
        stripe_count, tile_size, feature_width
    )

    return fused_layer(dense_cols, dense_edge_weights, dense_bands, sparse_w, incoming_rows, weight, bias)


def solution(mesh):
    placed = (
        P(AXES, None),
        P(AXES, None, None, None),
        P(AXES, None),
        P(),
        P(AXES, None),
        P(AXES, None, None),
        P(AXES, None),
        P(),
        P(),
    )
    return jax.shard_map(
        on_device, mesh=mesh, in_specs=placed, out_specs=P(AXES, None), check_vma=False
    )
```

```python
import functools

import jax
import jax.numpy as jnp
from jax import lax
from jax.experimental import pallas as pl
from jax.experimental.pallas import tpu as pltpu
from jax.sharding import PartitionSpec as P

AXES = ("row", "grp")


def gather_kernel(group, piece_ref, out_ref, send_sem, relay_sem, recv_sem, local_sem):
    n = out_ref.shape[0]
    chips = n // 2
    me = lax.axis_index(AXES)
    core = (me // group) % 2
    my_chip = (me // (2 * group)) * group + me % group
    mesh_ids = pl.DeviceIdType.MESH

    def device(chip, which_core):
        return ((chip // group) * 2 + which_core) * group + chip % group

    def where(k):
        return (k // group, k % group)

    def remote(src, dst, send, recv, k):
        return pltpu.make_async_remote_copy(
            src_ref=src, dst_ref=dst, send_sem=send, recv_sem=recv,
            device_id=where(k), device_id_type=mesh_ids,
        )

    partner = device(my_chip, 1 - core)
    barrier = pltpu.get_barrier_semaphore()
    pl.semaphore_signal(barrier, inc=1, device_id=where(partner), device_id_type=mesh_ids)

    def greet(i, carry):
        peer = device(lax.rem(my_chip + i, chips), core)
        pl.semaphore_signal(barrier, inc=1, device_id=where(peer), device_id_type=mesh_ids)
        return carry

    lax.fori_loop(1, chips, greet, 0)
    pl.semaphore_wait(barrier, chips)
    own = pltpu.make_async_copy(piece_ref, out_ref.at[me], local_sem)
    own.start()
    remote(piece_ref, out_ref.at[me], send_sem.at[0], recv_sem.at[me], partner).start()

    def send(i, carry):
        peer = device(lax.rem(my_chip + i, chips), core)
        remote(piece_ref, out_ref.at[me], send_sem.at[i], recv_sem.at[me], peer).start()
        return carry

    lax.fori_loop(1, chips, send, 0)

    def relay(i, carry):
        source = device(lax.rem(my_chip + chips - i, chips), core)
        remote(piece_ref, out_ref.at[source], send_sem.at[i], recv_sem.at[source], source).wait_recv()
        remote(out_ref.at[source], out_ref.at[source], relay_sem.at[i], recv_sem.at[source], partner).start()
        return carry

    lax.fori_loop(1, chips, relay, 0)
    remote(piece_ref, out_ref.at[partner], send_sem.at[0], recv_sem.at[partner], partner).wait_recv()

    def take(i, carry):
        source = device(lax.rem(my_chip + chips - i, chips), 1 - core)
        remote(piece_ref, out_ref.at[source], send_sem.at[i], recv_sem.at[source], partner).wait_recv()
        return carry

    lax.fori_loop(1, chips, take, 0)
    remote(piece_ref, out_ref.at[me], send_sem.at[0], recv_sem.at[me], partner).wait_send()

    def drain(i, carry):
        peer = device(lax.rem(my_chip + i, chips), core)
        remote(piece_ref, out_ref.at[me], send_sem.at[i], recv_sem.at[me], peer).wait_send()
        source = device(lax.rem(my_chip + chips - i, chips), core)
        remote(out_ref.at[source], out_ref.at[source], relay_sem.at[i], recv_sem.at[source], partner).wait_send()
        return carry

    lax.fori_loop(1, chips, drain, 0)
    own.wait()


def gather_pieces(piece, n, group):
    rows, width = piece.shape
    return pl.pallas_call(
        functools.partial(gather_kernel, group),
        out_shape=jax.ShapeDtypeStruct((n, rows, width), piece.dtype),
        in_specs=[pl.BlockSpec(memory_space=pltpu.VMEM)],
        out_specs=pl.BlockSpec(memory_space=pltpu.VMEM),
        scratch_shapes=[
            pltpu.SemaphoreType.DMA((n // 2,)),
            pltpu.SemaphoreType.DMA((n // 2,)),
            pltpu.SemaphoreType.DMA((n,)),
            pltpu.SemaphoreType.DMA,
        ],
        compiler_params=pltpu.CompilerParams(collective_id=0, has_side_effects=True),
    )(piece)

def layer_kernel(tiles_per, tile_size, step_blocks, cols_ref, w_ref, bands_ref, sw_ref, inc_ref, weight_ref, bias_ref, out_ref):
    step = pl.program_id(0)
    for half in range(step_blocks):
        rows = pl.ds(half * tile_size, tile_size)
        total = jnp.dot(sw_ref[rows], inc_ref[...], preferred_element_type=jnp.float32)
        for tile_index in range(tiles_per):
            col = cols_ref[(step * step_blocks + half) * tiles_per + tile_index]
            total = total + jnp.dot(w_ref[half, tile_index], bands_ref[col], preferred_element_type=jnp.float32)
        aggregate = total.astype(jnp.bfloat16)
        result = jnp.dot(aggregate, weight_ref[...], preferred_element_type=jnp.float32) + bias_ref[...]
        out_ref[rows] = jnp.maximum(result, 0.0).astype(out_ref.dtype)


def fused_layer(dense_cols, dense_edge_weights, dense_bands, sparse_w, incoming_rows, weight, bias):
    block_count, tiles_per, tile_size, _ = dense_edge_weights.shape
    stripe_count, _, width = dense_bands.shape
    slots = incoming_rows.shape[0]
    out_width = weight.shape[1]
    step_blocks = 2 if block_count % 2 == 0 else 1
    grid_spec = pltpu.PrefetchScalarGridSpec(
        num_scalar_prefetch=1,
        grid=(block_count // step_blocks,),
        in_specs=[
            pl.BlockSpec((step_blocks, tiles_per, tile_size, tile_size), lambda b, cols: (b, 0, 0, 0)),
            pl.BlockSpec(memory_space=pltpu.VMEM),
            pl.BlockSpec((step_blocks * tile_size, slots), lambda b, cols: (b, 0)),
            pl.BlockSpec(memory_space=pltpu.VMEM),
            pl.BlockSpec(memory_space=pltpu.VMEM),
            pl.BlockSpec(memory_space=pltpu.VMEM),
        ],
        out_specs=pl.BlockSpec((step_blocks * tile_size, out_width), lambda b, cols: (b, 0)),
    )
    return pl.pallas_call(
        functools.partial(layer_kernel, tiles_per, tile_size, step_blocks),
        grid_spec=grid_spec,
        out_shape=jax.ShapeDtypeStruct((block_count * tile_size, out_width), jnp.bfloat16),
    )(dense_cols.reshape(-1), dense_edge_weights, dense_bands, sparse_w, incoming_rows, weight, bias.reshape(1, -1))

def on_device(
    features,
    dense_edge_weights,
    dense_cols,
    dense_ids,
    sparse_w,
    sparse_rows,
    sparse_counts,
    weight,
    bias,
):
    block_count = dense_edge_weights.shape[0]
    tiles_per = dense_edge_weights.shape[1]
    tile_size = dense_edge_weights.shape[2]
    feature_width = features.shape[1]
    stripe_count = dense_ids.shape[0]
    local_blocks = features.reshape(block_count, tile_size, feature_width)
    group = lax.axis_size("grp")

    rows_out = sparse_rows[0]
    counts_out = sparse_counts[0]
    peer_count = rows_out.shape[0]
    slot_count = rows_out.shape[1]
    piece = stripe_count * tile_size // peer_count
    me = lax.axis_index(AXES)

    candidates = local_blocks[dense_ids % block_count]
    stripe_pieces = candidates.reshape(peer_count, piece, feature_width)

    stripe_arrived = lax.all_to_all(stripe_pieces, AXES, split_axis=0, concat_axis=0, tiled=True)
    my_owner = dense_ids[me * piece // tile_size] // block_count
    my_piece = lax.dynamic_index_in_dim(stripe_arrived, my_owner, 0, keepdims=False)

    outgoing = features[rows_out]
    slot_ids = jnp.arange(slot_count, dtype=jnp.int32)
    live_slots = slot_ids[None, :] < counts_out[:, None]
    outgoing = jnp.where(live_slots[:, :, None], outgoing, jnp.zeros((), outgoing.dtype))
    arrived = lax.all_to_all(outgoing, AXES, split_axis=0, concat_axis=0, tiled=True)
    incoming_rows = arrived.reshape(peer_count * slot_count, feature_width)
    dense_bands = gather_pieces(my_piece, peer_count, group).reshape(
        stripe_count, tile_size, feature_width
    )

    return fused_layer(dense_cols, dense_edge_weights, dense_bands, sparse_w, incoming_rows, weight, bias)


def solution(mesh):
    placed = (
        P(AXES, None),
        P(AXES, None, None, None),
        P(AXES, None),
        P(),
        P(AXES, None),
        P(AXES, None, None),
        P(AXES, None),
        P(),
        P(),
    )
    return jax.shard_map(
        on_device, mesh=mesh, in_specs=placed, out_specs=P(AXES, None), check_vma=False
    )
```

```python
import functools

import jax
import jax.numpy as jnp
from jax import lax
from jax.experimental import pallas as pl
from jax.experimental.pallas import tpu as pltpu
from jax.sharding import PartitionSpec as P

AXES = ("row", "grp")


def gather_kernel(group, piece_ref, out_ref, send_sem, relay_sem, recv_sem, local_sem):
    n = out_ref.shape[0]
    chips = n // 2
    me = lax.axis_index(AXES)
    core = (me // group) % 2
    my_chip = (me // (2 * group)) * group + me % group
    mesh_ids = pl.DeviceIdType.MESH

    def device(chip, which_core):
        return ((chip // group) * 2 + which_core) * group + chip % group

    def where(k):
        return (k // group, k % group)

    def remote(src, dst, send, recv, k):
        return pltpu.make_async_remote_copy(
            src_ref=src, dst_ref=dst, send_sem=send, recv_sem=recv,
            device_id=where(k), device_id_type=mesh_ids,
        )

    partner = device(my_chip, 1 - core)
    barrier = pltpu.get_barrier_semaphore()
    pl.semaphore_signal(barrier, inc=1, device_id=where(partner), device_id_type=mesh_ids)

    def greet(i, carry):
        peer = device(lax.rem(my_chip + i, chips), core)
        pl.semaphore_signal(barrier, inc=1, device_id=where(peer), device_id_type=mesh_ids)
        return carry

    lax.fori_loop(1, chips, greet, 0)
    pl.semaphore_wait(barrier, chips)
    own = pltpu.make_async_copy(piece_ref, out_ref.at[me], local_sem)
    own.start()
    remote(piece_ref, out_ref.at[me], send_sem.at[0], recv_sem.at[me], partner).start()

    def send(i, carry):
        peer = device(lax.rem(my_chip + i, chips), core)
        remote(piece_ref, out_ref.at[me], send_sem.at[i], recv_sem.at[me], peer).start()
        return carry

    lax.fori_loop(1, chips, send, 0)

    def relay(i, carry):
        source = device(lax.rem(my_chip + chips - i, chips), core)
        remote(piece_ref, out_ref.at[source], send_sem.at[i], recv_sem.at[source], source).wait_recv()
        remote(out_ref.at[source], out_ref.at[source], relay_sem.at[i], recv_sem.at[source], partner).start()
        return carry

    lax.fori_loop(1, chips, relay, 0)
    remote(piece_ref, out_ref.at[partner], send_sem.at[0], recv_sem.at[partner], partner).wait_recv()

    def take(i, carry):
        source = device(lax.rem(my_chip + chips - i, chips), 1 - core)
        remote(piece_ref, out_ref.at[source], send_sem.at[i], recv_sem.at[source], partner).wait_recv()
        return carry

    lax.fori_loop(1, chips, take, 0)
    remote(piece_ref, out_ref.at[me], send_sem.at[0], recv_sem.at[me], partner).wait_send()

    def drain(i, carry):
        peer = device(lax.rem(my_chip + i, chips), core)
        remote(piece_ref, out_ref.at[me], send_sem.at[i], recv_sem.at[me], peer).wait_send()
        source = device(lax.rem(my_chip + chips - i, chips), core)
        remote(out_ref.at[source], out_ref.at[source], relay_sem.at[i], recv_sem.at[source], partner).wait_send()
        return carry

    lax.fori_loop(1, chips, drain, 0)
    own.wait()


def gather_pieces(piece, n, group):
    rows, width = piece.shape
    return pl.pallas_call(
        functools.partial(gather_kernel, group),
        out_shape=jax.ShapeDtypeStruct((n, rows, width), piece.dtype),
        in_specs=[pl.BlockSpec(memory_space=pltpu.VMEM)],
        out_specs=pl.BlockSpec(memory_space=pltpu.VMEM),
        scratch_shapes=[
            pltpu.SemaphoreType.DMA((n // 2,)),
            pltpu.SemaphoreType.DMA((n // 2,)),
            pltpu.SemaphoreType.DMA((n,)),
            pltpu.SemaphoreType.DMA,
        ],
        compiler_params=pltpu.CompilerParams(collective_id=0, has_side_effects=True),
    )(piece)

def scatter_kernel(group, send_ref, out_ref, send_sem, recv_sem, local_sem):
    served = send_ref.shape[0]
    me = lax.axis_index(AXES)
    core = (me // group) % 2
    my_chip = (me // (2 * group)) * group + me % group
    parity = (core + my_chip) % 2
    mesh_ids = pl.DeviceIdType.MESH

    def device(chip, which_core):
        return ((chip // group) * 2 + which_core) * group + chip % group

    def where(k):
        return (k // group, k % group)

    def chip_of(m):
        return (m // 2) * group + (m % 2) * 2 + parity

    def remote(src, dst, send, recv, k):
        return pltpu.make_async_remote_copy(
            src_ref=src, dst_ref=dst, send_sem=send, recv_sem=recv,
            device_id=where(k), device_id_type=mesh_ids,
        )

    barrier = pltpu.get_barrier_semaphore()

    def greet(m, carry):
        peer = device(chip_of(m), core)

        @pl.when(peer != me)
        def _():
            pl.semaphore_signal(barrier, inc=1, device_id=where(peer), device_id_type=mesh_ids)

        return carry

    lax.fori_loop(0, served, greet, 0)

    pl.semaphore_wait(barrier, served - 1 + core)
    slot = my_chip // 2

    def send(m, carry):
        peer = device(chip_of(m), core)

        @pl.when(peer != me)
        def _():
            remote(send_ref.at[m], out_ref.at[slot], send_sem.at[m], recv_sem.at[slot], peer).start()

        @pl.when(peer == me)
        def _():
            pltpu.make_async_copy(send_ref.at[m], out_ref.at[slot], local_sem).start()

        return carry

    lax.fori_loop(0, served, send, 0)

    def wait(m, carry):
        sender = device(2 * m + parity, core)
        peer = device(chip_of(m), core)

        @pl.when(sender != me)
        def _():
            remote(send_ref.at[m], out_ref.at[m], send_sem.at[m], recv_sem.at[m], sender).wait_recv()

        @pl.when(sender == me)
        def _():
            pltpu.make_async_copy(send_ref.at[m], out_ref.at[m], local_sem).wait()

        @pl.when(peer != me)
        def _():
            remote(send_ref.at[m], out_ref.at[slot], send_sem.at[m], recv_sem.at[slot], peer).wait_send()

        return carry

    lax.fori_loop(0, served, wait, 0)


def scatter_pieces(send, group):
    return pl.pallas_call(
        functools.partial(scatter_kernel, group),
        out_shape=jax.ShapeDtypeStruct(send.shape, send.dtype),
        in_specs=[pl.BlockSpec(memory_space=pltpu.VMEM)],
        out_specs=pl.BlockSpec(memory_space=pltpu.VMEM),
        scratch_shapes=[
            pltpu.SemaphoreType.DMA((send.shape[0],)),
            pltpu.SemaphoreType.DMA((send.shape[0],)),
            pltpu.SemaphoreType.DMA,
        ],
        compiler_params=pltpu.CompilerParams(collective_id=1, has_side_effects=True),
    )(send)


def broadcast_stripes(local_blocks, dense_ids, n, group):
    block_count, tile_size, width = local_blocks.shape
    stripe_count = dense_ids.shape[0]
    piece = stripe_count * tile_size // n
    chips = n // 2
    me = lax.axis_index(AXES)
    row_count = lax.axis_size("row")
    core = (me // group) % 2
    my_chip = (me // (2 * group)) * group + me % group
    parity = (core + my_chip) % 2
    partner = me + group * (1 - 2 * core)
    swap = [(r, r ^ 1) for r in range(row_count)]

    def chip_of_device(k):
        return (k // (2 * group)) * group + k % group

    owners = dense_ids // block_count
    candidates = local_blocks[dense_ids % block_count].reshape(
        chips // group, 2, group // 2, 2, piece, width
    )
    mine = lax.dynamic_index_in_dim(candidates, parity, 3, keepdims=False)
    for_partner = lax.dynamic_index_in_dim(candidates, 1 - parity, 3, keepdims=False)
    from_partner = lax.ppermute(for_partner, "row", swap)
    z_part = jnp.arange(chips // group, dtype=jnp.int32)[:, None, None]
    c_part = jnp.arange(2, dtype=jnp.int32)[None, :, None]
    g_part = jnp.arange(group // 2, dtype=jnp.int32)[None, None, :]
    piece_ids = (z_part * 2 + c_part) * group + g_part * 2 + parity
    use_partner = owners[piece_ids * piece // tile_size] == partner
    chosen = jnp.where(use_partner[..., None, None], from_partner, mine)
    outgoing = jnp.transpose(chosen, (0, 2, 1, 3, 4)).reshape(chips // 2, 2 * piece, width)
    arrived = scatter_pieces(outgoing, group).reshape(chips // 2, 2, piece, width)

    def held(which_core):
        owner_chip = chip_of_device(owners[(me + group * (which_core - core)) * piece // tile_size])
        slot = lax.dynamic_index_in_dim(arrived, owner_chip // 2, 0, keepdims=False)
        return owner_chip % 2 == parity, lax.dynamic_index_in_dim(slot, which_core, 0, keepdims=False)

    _, to_partner = held(1 - core)
    mine_held, my_rows = held(core)
    got = lax.ppermute(to_partner, "row", swap)
    my_piece = jnp.where(mine_held, my_rows, got)
    return gather_pieces(my_piece, n, group).reshape(stripe_count, tile_size, width)


def layer_kernel(tiles_per, tile_size, step_blocks, cols_ref, w_ref, bands_ref, sw_ref, inc_ref, weight_ref, bias_ref, out_ref):
    step = pl.program_id(0)
    for half in range(step_blocks):
        rows = pl.ds(half * tile_size, tile_size)
        total = jnp.dot(sw_ref[rows], inc_ref[...], preferred_element_type=jnp.float32)
        for tile_index in range(tiles_per):
            col = cols_ref[(step * step_blocks + half) * tiles_per + tile_index]
            total = total + jnp.dot(w_ref[half, tile_index], bands_ref[col], preferred_element_type=jnp.float32)
        aggregate = total.astype(jnp.bfloat16)
        result = jnp.dot(aggregate, weight_ref[...], preferred_element_type=jnp.float32) + bias_ref[...]
        out_ref[rows] = jnp.maximum(result, 0.0).astype(out_ref.dtype)


def fused_layer(dense_cols, dense_edge_weights, dense_bands, sparse_w, incoming_rows, weight, bias):
    block_count, tiles_per, tile_size, _ = dense_edge_weights.shape
    stripe_count, _, width = dense_bands.shape
    slots = incoming_rows.shape[0]
    out_width = weight.shape[1]
    step_blocks = 2 if block_count % 2 == 0 else 1
    grid_spec = pltpu.PrefetchScalarGridSpec(
        num_scalar_prefetch=1,
        grid=(block_count // step_blocks,),
        in_specs=[
            pl.BlockSpec((step_blocks, tiles_per, tile_size, tile_size), lambda b, cols: (b, 0, 0, 0)),
            pl.BlockSpec((stripe_count, tile_size, width), lambda b, cols: (0, 0, 0)),
            pl.BlockSpec((step_blocks * tile_size, slots), lambda b, cols: (b, 0)),
            pl.BlockSpec((slots, width), lambda b, cols: (0, 0)),
            pl.BlockSpec((width, out_width), lambda b, cols: (0, 0)),
            pl.BlockSpec((1, out_width), lambda b, cols: (0, 0)),
        ],
        out_specs=pl.BlockSpec((step_blocks * tile_size, out_width), lambda b, cols: (b, 0)),
    )
    return pl.pallas_call(
        functools.partial(layer_kernel, tiles_per, tile_size, step_blocks),
        grid_spec=grid_spec,
        out_shape=jax.ShapeDtypeStruct((block_count * tile_size, out_width), jnp.bfloat16),
    )(dense_cols.reshape(-1), dense_edge_weights, dense_bands, sparse_w, incoming_rows, weight, bias.reshape(1, -1))

def on_device(
    features,
    dense_edge_weights,
    dense_cols,
    dense_ids,
    sparse_w,
    sparse_rows,
    sparse_counts,
    weight,
    bias,
):
    block_count = dense_edge_weights.shape[0]
    tiles_per = dense_edge_weights.shape[1]
    tile_size = dense_edge_weights.shape[2]
    feature_width = features.shape[1]
    stripe_count = dense_ids.shape[0]
    local_blocks = features.reshape(block_count, tile_size, feature_width)
    group = lax.axis_size("grp")

    rows_out = sparse_rows[0]
    counts_out = sparse_counts[0]
    peer_count = rows_out.shape[0]
    slot_count = rows_out.shape[1]
    piece = stripe_count * tile_size // peer_count
    me = lax.axis_index(AXES)

    dense_bands = broadcast_stripes(local_blocks, dense_ids, peer_count, group)

    outgoing = features[rows_out]
    slot_ids = jnp.arange(slot_count, dtype=jnp.int32)
    live_slots = slot_ids[None, :] < counts_out[:, None]
    outgoing = jnp.where(live_slots[:, :, None], outgoing, jnp.zeros((), outgoing.dtype))
    arrived = lax.all_to_all(outgoing, AXES, split_axis=0, concat_axis=0, tiled=True)
    incoming_rows = arrived.reshape(peer_count * slot_count, feature_width)

    return fused_layer(dense_cols, dense_edge_weights, dense_bands, sparse_w, incoming_rows, weight, bias)


def solution(mesh):
    placed = (
        P(AXES, None),
        P(AXES, None, None, None),
        P(AXES, None),
        P(),
        P(AXES, None),
        P(AXES, None, None),
        P(AXES, None),
        P(),
        P(),
    )
    return jax.shard_map(
        on_device, mesh=mesh, in_specs=placed, out_specs=P(AXES, None), check_vma=False
    )
```

```python
import functools

import jax
import jax.numpy as jnp
from jax import lax
from jax.experimental import pallas as pl
from jax.experimental.pallas import tpu as pltpu
from jax.sharding import PartitionSpec as P

AXES = ("row", "grp")


def gather_kernel(group, piece_ref, out_ref, send_sem, relay_sem, recv_sem, local_sem):
    n = out_ref.shape[0]
    chips = n // 2
    me = lax.axis_index(AXES)
    core = (me // group) % 2
    my_chip = (me // (2 * group)) * group + me % group
    mesh_ids = pl.DeviceIdType.MESH

    def device(chip, which_core):
        return ((chip // group) * 2 + which_core) * group + chip % group

    def where(k):
        return (k // group, k % group)

    def remote(src, dst, send, recv, k):
        return pltpu.make_async_remote_copy(
            src_ref=src, dst_ref=dst, send_sem=send, recv_sem=recv,
            device_id=where(k), device_id_type=mesh_ids,
        )

    partner = device(my_chip, 1 - core)
    barrier = pltpu.get_barrier_semaphore()
    pl.semaphore_signal(barrier, inc=1, device_id=where(partner), device_id_type=mesh_ids)

    def greet(i, carry):
        peer = device(lax.rem(my_chip + i, chips), core)
        pl.semaphore_signal(barrier, inc=1, device_id=where(peer), device_id_type=mesh_ids)
        return carry

    lax.fori_loop(1, chips, greet, 0)
    pl.semaphore_wait(barrier, chips)
    own = pltpu.make_async_copy(piece_ref, out_ref.at[me], local_sem)
    own.start()
    remote(piece_ref, out_ref.at[me], send_sem.at[0], recv_sem.at[me], partner).start()

    def send(i, carry):
        peer = device(lax.rem(my_chip + i, chips), core)
        remote(piece_ref, out_ref.at[me], send_sem.at[i], recv_sem.at[me], peer).start()
        return carry

    lax.fori_loop(1, chips, send, 0)

    def relay(i, carry):
        source = device(lax.rem(my_chip + chips - i, chips), core)
        remote(piece_ref, out_ref.at[source], send_sem.at[i], recv_sem.at[source], source).wait_recv()
        remote(out_ref.at[source], out_ref.at[source], relay_sem.at[i], recv_sem.at[source], partner).start()
        return carry

    lax.fori_loop(1, chips, relay, 0)
    remote(piece_ref, out_ref.at[partner], send_sem.at[0], recv_sem.at[partner], partner).wait_recv()

    def take(i, carry):
        source = device(lax.rem(my_chip + chips - i, chips), 1 - core)
        remote(piece_ref, out_ref.at[source], send_sem.at[i], recv_sem.at[source], partner).wait_recv()
        return carry

    lax.fori_loop(1, chips, take, 0)
    remote(piece_ref, out_ref.at[me], send_sem.at[0], recv_sem.at[me], partner).wait_send()

    def drain(i, carry):
        peer = device(lax.rem(my_chip + i, chips), core)
        remote(piece_ref, out_ref.at[me], send_sem.at[i], recv_sem.at[me], peer).wait_send()
        source = device(lax.rem(my_chip + chips - i, chips), core)
        remote(out_ref.at[source], out_ref.at[source], relay_sem.at[i], recv_sem.at[source], partner).wait_send()
        return carry

    lax.fori_loop(1, chips, drain, 0)
    own.wait()


def gather_pieces(piece, n, group):
    rows, width = piece.shape
    return pl.pallas_call(
        functools.partial(gather_kernel, group),
        out_shape=jax.ShapeDtypeStruct((n, rows, width), piece.dtype),
        in_specs=[pl.BlockSpec(memory_space=pltpu.VMEM)],
        out_specs=pl.BlockSpec(memory_space=pltpu.VMEM),
        scratch_shapes=[
            pltpu.SemaphoreType.DMA((n // 2,)),
            pltpu.SemaphoreType.DMA((n // 2,)),
            pltpu.SemaphoreType.DMA((n,)),
            pltpu.SemaphoreType.DMA,
        ],
        compiler_params=pltpu.CompilerParams(collective_id=0, has_side_effects=True),
    )(piece)

def layer_kernel(tiles_per, tile_size, step_blocks, cols_ref, w_ref, bands_ref, sw_ref, inc_ref, weight_ref, bias_ref, out_ref):
    step = pl.program_id(0)
    for half in range(step_blocks):
        rows = pl.ds(half * tile_size, tile_size)
        total = jnp.dot(sw_ref[rows], inc_ref[...], preferred_element_type=jnp.float32)
        for tile_index in range(tiles_per):
            col = cols_ref[tile_index, step * step_blocks + half]
            total = total + jnp.dot(w_ref[half, tile_index], bands_ref[col], preferred_element_type=jnp.float32)
        aggregate = total.astype(jnp.bfloat16)
        result = jnp.dot(aggregate, weight_ref[...], preferred_element_type=jnp.float32) + bias_ref[...]
        out_ref[rows] = jnp.maximum(result, 0.0).astype(out_ref.dtype)


def fused_layer(dense_cols, dense_edge_weights, dense_bands, sparse_w, incoming_rows, weight, bias):
    block_count, tiles_per, tile_size, _ = dense_edge_weights.shape
    stripe_count, _, width = dense_bands.shape
    slots = incoming_rows.shape[0]
    out_width = weight.shape[1]
    step_blocks = 2 if block_count % 2 == 0 else 1
    grid_spec = pltpu.PrefetchScalarGridSpec(
        num_scalar_prefetch=1,
        grid=(block_count // step_blocks,),
        in_specs=[
            pl.BlockSpec((step_blocks, tiles_per, tile_size, tile_size), lambda b, cols: (b, 0, 0, 0)),
            pl.BlockSpec(memory_space=pltpu.VMEM),
            pl.BlockSpec((step_blocks * tile_size, slots), lambda b, cols: (b, 0)),
            pl.BlockSpec(memory_space=pltpu.VMEM),
            pl.BlockSpec(memory_space=pltpu.VMEM),
            pl.BlockSpec(memory_space=pltpu.VMEM),
        ],
        out_specs=pl.BlockSpec((step_blocks * tile_size, out_width), lambda b, cols: (b, 0)),
    )
    return pl.pallas_call(
        functools.partial(layer_kernel, tiles_per, tile_size, step_blocks),
        grid_spec=grid_spec,
        out_shape=jax.ShapeDtypeStruct((block_count * tile_size, out_width), jnp.bfloat16),
    )(dense_cols.T, dense_edge_weights, dense_bands, sparse_w, incoming_rows, weight, bias)

def on_device(
    features,
    dense_edge_weights,
    dense_cols,
    dense_ids,
    sparse_w,
    sparse_rows,
    sparse_counts,
    weight,
    bias,
):
    block_count = dense_edge_weights.shape[0]
    tiles_per = dense_edge_weights.shape[1]
    tile_size = dense_edge_weights.shape[2]
    feature_width = features.shape[1]
    stripe_count = dense_ids.shape[0]
    local_blocks = features.reshape(block_count, tile_size, feature_width)
    group = lax.axis_size("grp")

    rows_out = sparse_rows[0]
    counts_out = sparse_counts[0]
    peer_count = rows_out.shape[0]
    slot_count = rows_out.shape[1]
    piece = stripe_count * tile_size // peer_count
    me = lax.axis_index(AXES)

    candidates = local_blocks[dense_ids % block_count]
    stripe_pieces = candidates.reshape(peer_count, piece, feature_width)

    stripe_arrived = lax.all_to_all(stripe_pieces, AXES, split_axis=0, concat_axis=0, tiled=True)
    stripe_ids = jnp.arange(stripe_count, dtype=jnp.int32)
    my_owner = jnp.sum(jnp.where(stripe_ids == me * piece // tile_size, dense_ids, 0)) // block_count
    from_owner = jnp.arange(peer_count, dtype=jnp.int32) == my_owner
    my_piece = jnp.sum(
        jnp.where(from_owner[:, None, None], stripe_arrived, jnp.zeros((), stripe_arrived.dtype)).astype(jnp.float32),
        axis=0,
    ).astype(stripe_arrived.dtype)

    outgoing = features[rows_out]
    slot_ids = jnp.arange(slot_count, dtype=jnp.int32)
    live_slots = slot_ids[None, :] < counts_out[:, None]
    outgoing = jnp.where(live_slots[:, :, None], outgoing, jnp.zeros((), outgoing.dtype))
    arrived = lax.all_to_all(outgoing, AXES, split_axis=0, concat_axis=0, tiled=True)
    incoming_rows = arrived.reshape(peer_count * slot_count, feature_width)
    dense_bands = gather_pieces(my_piece, peer_count, group).reshape(
        stripe_count, tile_size, feature_width
    )

    return fused_layer(dense_cols, dense_edge_weights, dense_bands, sparse_w, incoming_rows, weight, bias)


def solution(mesh):
    placed = (
        P(AXES, None),
        P(AXES, None, None, None),
        P(AXES, None),
        P(),
        P(AXES, None),
        P(AXES, None, None),
        P(AXES, None),
        P(),
        P(),
    )
    return jax.shard_map(
        on_device, mesh=mesh, in_specs=placed, out_specs=P(AXES, None), check_vma=False
    )
```

```python
import functools

import jax
import jax.numpy as jnp
from jax import lax
from jax.experimental import pallas as pl
from jax.experimental.pallas import tpu as pltpu
from jax.sharding import PartitionSpec as P

AXES = ("row", "grp")


def gather_kernel(group, piece_ref, out_ref, send_sem, relay_sem, recv_sem, local_sem):
    n = out_ref.shape[0]
    chips = n // 2
    me = lax.axis_index(AXES)
    core = (me // group) % 2
    my_chip = (me // (2 * group)) * group + me % group
    mesh_ids = pl.DeviceIdType.MESH

    def device(chip, which_core):
        return ((chip // group) * 2 + which_core) * group + chip % group

    def where(k):
        return (k // group, k % group)

    def remote(src, dst, send, recv, k):
        return pltpu.make_async_remote_copy(
            src_ref=src, dst_ref=dst, send_sem=send, recv_sem=recv,
            device_id=where(k), device_id_type=mesh_ids,
        )

    partner = device(my_chip, 1 - core)
    barrier = pltpu.get_barrier_semaphore()
    pl.semaphore_signal(barrier, inc=1, device_id=where(partner), device_id_type=mesh_ids)

    def greet(i, carry):
        peer = device(lax.rem(my_chip + i, chips), core)
        pl.semaphore_signal(barrier, inc=1, device_id=where(peer), device_id_type=mesh_ids)
        return carry

    lax.fori_loop(1, chips, greet, 0)
    pl.semaphore_wait(barrier, chips)
    own = pltpu.make_async_copy(piece_ref, out_ref.at[me], local_sem)
    own.start()
    remote(piece_ref, out_ref.at[me], send_sem.at[0], recv_sem.at[me], partner).start()

    def send(i, carry):
        peer = device(lax.rem(my_chip + i, chips), core)
        remote(piece_ref, out_ref.at[me], send_sem.at[i], recv_sem.at[me], peer).start()
        return carry

    lax.fori_loop(1, chips, send, 0)

    def relay(i, carry):
        source = device(lax.rem(my_chip + chips - i, chips), core)
        remote(piece_ref, out_ref.at[source], send_sem.at[i], recv_sem.at[source], source).wait_recv()
        remote(out_ref.at[source], out_ref.at[source], relay_sem.at[i], recv_sem.at[source], partner).start()
        return carry

    lax.fori_loop(1, chips, relay, 0)
    remote(piece_ref, out_ref.at[partner], send_sem.at[0], recv_sem.at[partner], partner).wait_recv()

    def take(i, carry):
        source = device(lax.rem(my_chip + chips - i, chips), 1 - core)
        remote(piece_ref, out_ref.at[source], send_sem.at[i], recv_sem.at[source], partner).wait_recv()
        return carry

    lax.fori_loop(1, chips, take, 0)
    remote(piece_ref, out_ref.at[me], send_sem.at[0], recv_sem.at[me], partner).wait_send()

    def drain(i, carry):
        peer = device(lax.rem(my_chip + i, chips), core)
        remote(piece_ref, out_ref.at[me], send_sem.at[i], recv_sem.at[me], peer).wait_send()
        source = device(lax.rem(my_chip + chips - i, chips), core)
        remote(out_ref.at[source], out_ref.at[source], relay_sem.at[i], recv_sem.at[source], partner).wait_send()
        return carry

    lax.fori_loop(1, chips, drain, 0)
    own.wait()


def gather_pieces(piece, n, group):
    rows, width = piece.shape
    return pl.pallas_call(
        functools.partial(gather_kernel, group),
        out_shape=jax.ShapeDtypeStruct((n, rows, width), piece.dtype),
        in_specs=[pl.BlockSpec(memory_space=pltpu.VMEM)],
        out_specs=pl.BlockSpec(memory_space=pltpu.VMEM),
        scratch_shapes=[
            pltpu.SemaphoreType.DMA((n // 2,)),
            pltpu.SemaphoreType.DMA((n // 2,)),
            pltpu.SemaphoreType.DMA((n,)),
            pltpu.SemaphoreType.DMA,
        ],
        compiler_params=pltpu.CompilerParams(collective_id=0, has_side_effects=True),
    )(piece)

def dimgather_kernel(group, piece_ref, out_ref, s1, r1, s2, r2, s3, r3, s4, r4, local_sem):
    Z, X, C, Y = out_ref.shape[:4]
    me = lax.axis_index(AXES)
    row = me // group
    y = me % group
    core = row % 2
    x = (row // 2) % X
    z = row // (2 * X)
    MESH = pl.DeviceIdType.MESH
    def did(zz, xx, cc, yy):
        return ((zz * X + xx) * 2 + cc, yy)
    def rc(src, dst, ss, rs, dev):
        return pltpu.make_async_remote_copy(src_ref=src, dst_ref=dst, send_sem=ss, recv_sem=rs, device_id=dev, device_id_type=MESH)
    barrier = pltpu.get_barrier_semaphore()
    peers = [did(z, x, core, (y + d) % Y) for d in range(1, Y)] + [did(z, (x + d) % X, core, y) for d in range(1, X)] \
        + [did((z + d) % Z, x, core, y) for d in range(1, Z)] + [did(z, x, 1 - core, y)]
    for p in peers:
        pl.semaphore_signal(barrier, inc=1, device_id=p, device_id_type=MESH)
    pl.semaphore_wait(barrier, len(peers))
    own = pltpu.make_async_copy(piece_ref, out_ref.at[z, x, core, y], local_sem)
    own.start()
    partner = did(z, x, 1 - core, y)
    for d in range(1, Y):
        rc(piece_ref, out_ref.at[z, x, core, y], s1.at[d], r1.at[y], did(z, x, core, (y + d) % Y)).start()
    for d in range(1, Y):
        ys = (y + Y - d) % Y
        rc(piece_ref, out_ref.at[z, x, core, ys], s1.at[d], r1.at[ys], did(z, x, core, ys)).wait_recv()
    own.wait()
    for d in range(1, X):
        rc(out_ref.at[z, x, core], out_ref.at[z, x, core], s2.at[d], r2.at[x], did(z, (x + d) % X, core, y)).start()
    rc(out_ref.at[z, x, core], out_ref.at[z, x, core], s4.at[z * X + x], r4.at[z * X + x], partner).start()
    for d in range(1, X):
        xs = (x + X - d) % X
        rc(out_ref.at[z, xs, core], out_ref.at[z, xs, core], s2.at[d], r2.at[xs], did(z, xs, core, y)).wait_recv()
        rc(out_ref.at[z, xs, core], out_ref.at[z, xs, core], s4.at[z * X + xs], r4.at[z * X + xs], partner).start()
    for d in range(1, Z):
        for xx in range(X):
            rc(out_ref.at[z, xx, core], out_ref.at[z, xx, core], s3.at[d * X + xx], r3.at[z * X + xx], did((z + d) % Z, x, core, y)).start()
    for d in range(1, Z):
        zs = (z + Z - d) % Z
        for xx in range(X):
            rc(out_ref.at[zs, xx, core], out_ref.at[zs, xx, core], s3.at[d * X + xx], r3.at[zs * X + xx], did(zs, x, core, y)).wait_recv()
            rc(out_ref.at[zs, xx, core], out_ref.at[zs, xx, core], s4.at[zs * X + xx], r4.at[zs * X + xx], partner).start()
    for zz in range(Z):
        for xx in range(X):
            rc(out_ref.at[zz, xx, 1 - core], out_ref.at[zz, xx, 1 - core], s4.at[zz * X + xx], r4.at[zz * X + xx], partner).wait_recv()
    for d in range(1, Y):
        rc(piece_ref, out_ref.at[z, x, core, y], s1.at[d], r1.at[y], did(z, x, core, (y + d) % Y)).wait_send()
    for d in range(1, X):
        rc(out_ref.at[z, x, core], out_ref.at[z, x, core], s2.at[d], r2.at[x], did(z, (x + d) % X, core, y)).wait_send()
    for d in range(1, Z):
        for xx in range(X):
            rc(out_ref.at[z, xx, core], out_ref.at[z, xx, core], s3.at[d * X + xx], r3.at[z * X + xx], did((z + d) % Z, x, core, y)).wait_send()
    for zz in range(Z):
        for xx in range(X):
            rc(out_ref.at[zz, xx, core], out_ref.at[zz, xx, core], s4.at[zz * X + xx], r4.at[zz * X + xx], partner).wait_send()

def dim_gather(piece, row_count, group):
    rows, width = piece.shape
    across = 4 if (row_count // 2) % 4 == 0 else 1
    depth = row_count // 2 // across
    sem = pltpu.SemaphoreType.DMA
    return pl.pallas_call(
        functools.partial(dimgather_kernel, group),
        out_shape=jax.ShapeDtypeStruct((depth, across, 2, group, rows, width), piece.dtype),
        in_specs=[pl.BlockSpec(memory_space=pltpu.VMEM)],
        out_specs=pl.BlockSpec(memory_space=pltpu.VMEM),
        scratch_shapes=[
            sem((group,)), sem((group,)), sem((across,)), sem((across,)),
            sem((depth * across,)), sem((depth * across,)), sem((depth * across,)), sem((depth * across,)), sem,
        ],
        compiler_params=pltpu.CompilerParams(collective_id=0, has_side_effects=True),
    )(piece)


def layer_kernel(tiles_per, tile_size, step_blocks, cols_ref, w_ref, bands_ref, sw_ref, inc_ref, weight_ref, bias_ref, out_ref):
    step = pl.program_id(0)
    for half in range(step_blocks):
        rows = pl.ds(half * tile_size, tile_size)
        total = jnp.dot(sw_ref[rows], inc_ref[...], preferred_element_type=jnp.float32)
        for tile_index in range(tiles_per):
            col = cols_ref[(step * step_blocks + half) * tiles_per + tile_index]
            total = total + jnp.dot(w_ref[half, tile_index], bands_ref[col], preferred_element_type=jnp.float32)
        aggregate = total.astype(jnp.bfloat16)
        result = jnp.dot(aggregate, weight_ref[...], preferred_element_type=jnp.float32) + bias_ref[...]
        out_ref[rows] = jnp.maximum(result, 0.0).astype(out_ref.dtype)


def fused_layer(dense_cols, dense_edge_weights, dense_bands, sparse_w, incoming_rows, weight, bias):
    block_count, tiles_per, tile_size, _ = dense_edge_weights.shape
    stripe_count, _, width = dense_bands.shape
    slots = incoming_rows.shape[0]
    out_width = weight.shape[1]
    step_blocks = 2 if block_count % 2 == 0 else 1
    grid_spec = pltpu.PrefetchScalarGridSpec(
        num_scalar_prefetch=1,
        grid=(block_count // step_blocks,),
        in_specs=[
            pl.BlockSpec((step_blocks, tiles_per, tile_size, tile_size), lambda b, cols: (b, 0, 0, 0)),
            pl.BlockSpec(memory_space=pltpu.VMEM),
            pl.BlockSpec((step_blocks * tile_size, slots), lambda b, cols: (b, 0)),
            pl.BlockSpec(memory_space=pltpu.VMEM),
            pl.BlockSpec(memory_space=pltpu.VMEM),
            pl.BlockSpec(memory_space=pltpu.VMEM),
        ],
        out_specs=pl.BlockSpec((step_blocks * tile_size, out_width), lambda b, cols: (b, 0)),
    )
    return pl.pallas_call(
        functools.partial(layer_kernel, tiles_per, tile_size, step_blocks),
        grid_spec=grid_spec,
        out_shape=jax.ShapeDtypeStruct((block_count * tile_size, out_width), jnp.bfloat16),
    )(dense_cols.reshape(-1), dense_edge_weights, dense_bands, sparse_w, incoming_rows, weight, bias.reshape(1, -1))

def on_device(
    features,
    dense_edge_weights,
    dense_cols,
    dense_ids,
    sparse_w,
    sparse_rows,
    sparse_counts,
    weight,
    bias,
):
    block_count = dense_edge_weights.shape[0]
    tiles_per = dense_edge_weights.shape[1]
    tile_size = dense_edge_weights.shape[2]
    feature_width = features.shape[1]
    stripe_count = dense_ids.shape[0]
    local_blocks = features.reshape(block_count, tile_size, feature_width)
    group = lax.axis_size("grp")

    rows_out = sparse_rows[0]
    counts_out = sparse_counts[0]
    peer_count = rows_out.shape[0]
    slot_count = rows_out.shape[1]
    piece = stripe_count * tile_size // peer_count
    me = lax.axis_index(AXES)

    candidates = local_blocks[dense_ids % block_count]
    stripe_pieces = candidates.reshape(peer_count, piece, feature_width)

    stripe_arrived = lax.all_to_all(stripe_pieces, AXES, split_axis=0, concat_axis=0, tiled=True)
    my_owner = dense_ids[me * piece // tile_size] // block_count
    my_piece = lax.dynamic_index_in_dim(stripe_arrived, my_owner, 0, keepdims=False)

    outgoing = features[rows_out]
    slot_ids = jnp.arange(slot_count, dtype=jnp.int32)
    live_slots = slot_ids[None, :] < counts_out[:, None]
    outgoing = jnp.where(live_slots[:, :, None], outgoing, jnp.zeros((), outgoing.dtype))
    arrived = lax.all_to_all(outgoing, AXES, split_axis=0, concat_axis=0, tiled=True)
    incoming_rows = arrived.reshape(peer_count * slot_count, feature_width)
    dense_bands = dim_gather(my_piece, lax.axis_size("row"), group).reshape(
        stripe_count, tile_size, feature_width
    )

    return fused_layer(dense_cols, dense_edge_weights, dense_bands, sparse_w, incoming_rows, weight, bias)


def solution(mesh):
    placed = (
        P(AXES, None),
        P(AXES, None, None, None),
        P(AXES, None),
        P(),
        P(AXES, None),
        P(AXES, None, None),
        P(AXES, None),
        P(),
        P(),
    )
    return jax.shard_map(
        on_device, mesh=mesh, in_specs=placed, out_specs=P(AXES, None), check_vma=False
    )
```

```python
import functools

import jax
import jax.numpy as jnp
from jax import lax
from jax.experimental import pallas as pl
from jax.experimental.pallas import tpu as pltpu
from jax.sharding import PartitionSpec as P

AXES = ("row", "grp")


def gather_kernel(group, piece_ref, out_ref, send_sem, relay_sem, recv_sem, local_sem):
    n = out_ref.shape[0]
    chips = n // 2
    me = lax.axis_index(AXES)
    core = (me // group) % 2
    my_chip = (me // (2 * group)) * group + me % group
    mesh_ids = pl.DeviceIdType.MESH

    def device(chip, which_core):
        return ((chip // group) * 2 + which_core) * group + chip % group

    def where(k):
        return (k // group, k % group)

    def remote(src, dst, send, recv, k):
        return pltpu.make_async_remote_copy(
            src_ref=src, dst_ref=dst, send_sem=send, recv_sem=recv,
            device_id=where(k), device_id_type=mesh_ids,
        )

    partner = device(my_chip, 1 - core)
    barrier = pltpu.get_barrier_semaphore()
    pl.semaphore_signal(barrier, inc=1, device_id=where(partner), device_id_type=mesh_ids)

    def greet(i, carry):
        peer = device(lax.rem(my_chip + i, chips), core)
        pl.semaphore_signal(barrier, inc=1, device_id=where(peer), device_id_type=mesh_ids)
        return carry

    lax.fori_loop(1, chips, greet, 0)
    pl.semaphore_wait(barrier, chips)
    own = pltpu.make_async_copy(piece_ref, out_ref.at[me], local_sem)
    own.start()
    remote(piece_ref, out_ref.at[me], send_sem.at[0], recv_sem.at[me], partner).start()

    def send(i, carry):
        peer = device(lax.rem(my_chip + i, chips), core)
        remote(piece_ref, out_ref.at[me], send_sem.at[i], recv_sem.at[me], peer).start()
        return carry

    lax.fori_loop(1, chips, send, 0)

    def relay(i, carry):
        source = device(lax.rem(my_chip + chips - i, chips), core)
        remote(piece_ref, out_ref.at[source], send_sem.at[i], recv_sem.at[source], source).wait_recv()
        remote(out_ref.at[source], out_ref.at[source], relay_sem.at[i], recv_sem.at[source], partner).start()
        return carry

    lax.fori_loop(1, chips, relay, 0)
    remote(piece_ref, out_ref.at[partner], send_sem.at[0], recv_sem.at[partner], partner).wait_recv()

    def take(i, carry):
        source = device(lax.rem(my_chip + chips - i, chips), 1 - core)
        remote(piece_ref, out_ref.at[source], send_sem.at[i], recv_sem.at[source], partner).wait_recv()
        return carry

    lax.fori_loop(1, chips, take, 0)
    remote(piece_ref, out_ref.at[me], send_sem.at[0], recv_sem.at[me], partner).wait_send()

    def drain(i, carry):
        peer = device(lax.rem(my_chip + i, chips), core)
        remote(piece_ref, out_ref.at[me], send_sem.at[i], recv_sem.at[me], peer).wait_send()
        source = device(lax.rem(my_chip + chips - i, chips), core)
        remote(out_ref.at[source], out_ref.at[source], relay_sem.at[i], recv_sem.at[source], partner).wait_send()
        return carry

    lax.fori_loop(1, chips, drain, 0)
    own.wait()


def gather_pieces(piece, n, group):
    rows, width = piece.shape
    return pl.pallas_call(
        functools.partial(gather_kernel, group),
        out_shape=jax.ShapeDtypeStruct((n, rows, width), piece.dtype),
        in_specs=[pl.BlockSpec(memory_space=pltpu.VMEM)],
        out_specs=pl.BlockSpec(memory_space=pltpu.VMEM),
        scratch_shapes=[
            pltpu.SemaphoreType.DMA((n // 2,)),
            pltpu.SemaphoreType.DMA((n // 2,)),
            pltpu.SemaphoreType.DMA((n,)),
            pltpu.SemaphoreType.DMA,
        ],
        compiler_params=pltpu.CompilerParams(collective_id=0, has_side_effects=True),
    )(piece)

def layer_kernel(tiles_per, tile_size, step_blocks, cols_ref, w_ref, bands_ref, sw_ref, inc_ref, weight_ref, bias_ref, out_ref):
    step = pl.program_id(0)
    for half in range(step_blocks):
        rows = pl.ds(half * tile_size, tile_size)
        total = jnp.dot(sw_ref[rows], inc_ref[...], preferred_element_type=jnp.float32)
        for tile_index in range(tiles_per):
            col = cols_ref[tile_index, step * step_blocks + half]
            total = total + jnp.dot(w_ref[half, tile_index], bands_ref[col], preferred_element_type=jnp.float32)
        aggregate = total.astype(jnp.bfloat16)
        result = jnp.dot(aggregate, weight_ref[...], preferred_element_type=jnp.float32) + bias_ref[...]
        out_ref[rows] = jnp.maximum(result, 0.0).astype(out_ref.dtype)


def fused_layer(dense_cols, dense_edge_weights, dense_bands, sparse_w, incoming_rows, weight, bias):
    block_count, tiles_per, tile_size, _ = dense_edge_weights.shape
    stripe_count, _, width = dense_bands.shape
    slots = incoming_rows.shape[0]
    out_width = weight.shape[1]
    step_blocks = 2 if block_count % 2 == 0 else 1
    grid_spec = pltpu.PrefetchScalarGridSpec(
        num_scalar_prefetch=1,
        grid=(block_count // step_blocks,),
        in_specs=[
            pl.BlockSpec((step_blocks, tiles_per, tile_size, tile_size), lambda b, cols: (b, 0, 0, 0)),
            pl.BlockSpec(memory_space=pltpu.VMEM),
            pl.BlockSpec((step_blocks * tile_size, slots), lambda b, cols: (b, 0)),
            pl.BlockSpec(memory_space=pltpu.VMEM),
            pl.BlockSpec(memory_space=pltpu.VMEM),
            pl.BlockSpec(memory_space=pltpu.VMEM),
        ],
        out_specs=pl.BlockSpec((step_blocks * tile_size, out_width), lambda b, cols: (b, 0)),
    )
    return pl.pallas_call(
        functools.partial(layer_kernel, tiles_per, tile_size, step_blocks),
        grid_spec=grid_spec,
        out_shape=jax.ShapeDtypeStruct((block_count * tile_size, out_width), jnp.bfloat16),
    )(dense_cols.T, dense_edge_weights, dense_bands, sparse_w, incoming_rows, weight, bias)

def on_device(
    features,
    dense_edge_weights,
    dense_cols,
    dense_ids,
    sparse_w,
    sparse_rows,
    sparse_counts,
    weight,
    bias,
):
    block_count = dense_edge_weights.shape[0]
    tiles_per = dense_edge_weights.shape[1]
    tile_size = dense_edge_weights.shape[2]
    feature_width = features.shape[1]
    stripe_count = dense_ids.shape[0]
    local_blocks = features.reshape(block_count, tile_size, feature_width)
    group = lax.axis_size("grp")

    rows_out = sparse_rows[0]
    counts_out = sparse_counts[0]
    peer_count = rows_out.shape[0]
    slot_count = rows_out.shape[1]
    piece = stripe_count * tile_size // peer_count
    me = lax.axis_index(AXES)

    candidates = local_blocks[dense_ids % block_count]
    stripe_pieces = candidates.reshape(peer_count, piece, feature_width)

    stripe_arrived = lax.all_to_all(stripe_pieces, AXES, split_axis=0, concat_axis=0, tiled=True)
    my_owner = dense_ids[me * piece // tile_size] // block_count
    my_piece = lax.dynamic_index_in_dim(stripe_arrived, my_owner, 0, keepdims=False)

    outgoing = features[rows_out]
    slot_ids = jnp.arange(slot_count, dtype=jnp.int32)
    live_slots = slot_ids[None, :] < counts_out[:, None]
    outgoing = jnp.where(live_slots[:, :, None], outgoing, jnp.zeros((), outgoing.dtype))
    arrived = lax.all_to_all(outgoing, AXES, split_axis=0, concat_axis=0, tiled=True)
    incoming_rows = arrived.reshape(peer_count * slot_count, feature_width)
    dense_bands = gather_pieces(my_piece, peer_count, group).reshape(
        stripe_count, tile_size, feature_width
    )

    return fused_layer(dense_cols, dense_edge_weights, dense_bands, sparse_w, incoming_rows, weight, bias)


def solution(mesh):
    placed = (
        P(AXES, None),
        P(AXES, None, None, None),
        P(AXES, None),
        P(),
        P(AXES, None),
        P(AXES, None, None),
        P(AXES, None),
        P(),
        P(),
    )
    return jax.shard_map(
        on_device, mesh=mesh, in_specs=placed, out_specs=P(AXES, None), check_vma=False
    )
```
